32 devices in a mesh: shard: 8 (over y, x, core), rep: 4 (over z).
Axes of the slice: x: 2, y: 2, z: 4, core: 2. Of those that a mesh axis runs over, the one named last changes fastest.
Arguments:
- inputs: float32 [8192, 768], P(('shard', 'rep')), may hold values from -6 to 6
- image_ids: int32 [8192], P(('shard', 'rep')), may hold values from 0 to 50, never falling along the last dimension, each value on 1 to 197 neighbouring positions
- output_gradient: float32 [8192, 768], P(('shard', 'rep')), may hold values from -6 to 6
- first_norm_scale: float32 [768], P('shard'), may hold values from 0.5 to 1.5
- first_norm_bias: float32 [768], P('shard'), may hold values from -1.5 to 1.5
- w_qkv: float32 [768, 2304], P('shard'), may hold values from -0.45 to 0.45
- bias_query: float32 [768], P('shard'), may hold values from -1.5 to 1.5
- bias_value: float32 [768], P('shard'), may hold values from -1.5 to 1.5
- w_output: float32 [768, 768], P('shard'), may hold values from -1.75 to 1.75
- bias_output: float32 [768], P('shard'), may hold values from -1.5 to 1.5
- second_norm_scale: float32 [768], P('shard'), may hold values from 0.5 to 1.5
- second_norm_bias: float32 [768], P('shard'), may hold values from -1.5 to 1.5
- w_up: float32 [768, 3072], P('shard'), may hold values from -0.21875 to 0.21875
- bias_up: float32 [3072], P('shard'), may hold values from -1.5 to 1.5
- w_down: float32 [3072, 768], P(None, 'shard'), may hold values from -0.109375 to 0.109375
- bias_down: float32 [768], P('shard'), may hold values from -1.5 to 1.5
Outputs:
- outputs: float32 [8192, 768], P(('shard', 'rep'))
- gradient_of_input: float32 [8192, 768], P(('shard', 'rep'))
- gradient_first_norm_scale: float32 [768], P('shard')
- grad_norm1_bias: float32 [768], P('shard')
- grad_w_qkv: float32 [768, 2304], P('shard')
- grad_bias_query: float32 [768], P('shard')
- grad_bias_value: float32 [768], P('shard')
- grad_w_output: float32 [768, 768], P('shard')
- grad_bias_output: float32 [768], P('shard')
- gradient_second_norm_scale: float32 [768], P('shard')
- grad_norm2_bias: float32 [768], P('shard')
- grad_w_up: float32 [768, 3072], P('shard')
- grad_bias_up: float32 [3072], P('shard')
- grad_w_down: float32 [3072, 768], P(None, 'shard')
- grad_bias_down: float32 [768], P('shard')
The draws below stay inside these ranges and needn't reach their ends.
Inputs may be any that keep to these rules, and one draw needn't show every extreme that they name: `image_ids`: image ids never fall from one slot to the next; each image holds 1 to 197 consecutive slots, and some image exactly 197.
All inputs are finite; a program needn't handle non-finite values.
Results may differ from the reference program's by a relative error of at most 0.0003.
Values sent between devices are 32-bit elements; how exact they have to be, the bound alone decides.
No kernel may reach another device: no remote copies, remote signals or barrier semaphores. Data moves between devices by JAX's collectives and lax.ppermute only.
A program may use at most 192 MiB of HBM per device.

```python
import math
import jax
import jax.numpy as jnp
import numpy as np
from jax import lax

D = 768
HEADS = 12
FF = 3072
TOK_DEV = 256
MAXLEN = 197
HALO = 256
TOKENS = 8192
IMAGES = 51


def draw_inputs(key, part):
    return jnp.clip(jax.random.normal(key, (TOKENS, D), jnp.float32), -6.0, 6.0)


def draw_w_qkv(key, part):
    spread = D ** (-0.5)
    bound = min(6.0 * spread, 0.45)
    return jnp.clip(jax.random.normal(key, (D, 3 * D), jnp.float32) * spread, -bound, bound)


def raised(values, stream_key, source, target, shards_of, factor):
    owner, partner = [(jnp.arange(values.shape[position]) // (values.shape[position] // shards_of)).reshape([-1 if axis == position else 1 for axis in range(values.ndim)]) for position in (source, target)]
    chosen = jax.random.permutation(stream_key, shards_of)[partner]
    strong = (owner == chosen) | (owner == (partner + shards_of // 2) % shards_of)
    return jnp.where(strong, factor * values, values)


def block_scale(stream_key, shape, pieces, smallest, high):
    factor_of, own = 1.0, jax.random.fold_in(stream_key, 6)
    for position, shards_of in pieces:
        heights = jnp.exp(jax.random.uniform(jax.random.fold_in(own, position), (shards_of,), jnp.float32, smallest / len(pieces), high / len(pieces)))
        factor_of = factor_of * jnp.repeat(heights, shape[position] // shards_of).reshape([-1 if axis == position else 1 for axis in range(len(shape))])
    return factor_of


def length_profile(amount, total, most, lean):
    weights = [(1 << 20) // math.isqrt(grade ** lean) + 1 for grade in range(2, amount + 1)]
    rest, holding = total - most - (amount - 1), [1] * (amount - 1)
    while rest > 0:
        candidates = [i for i in range(amount - 1) if holding[i] < most]
        pool, remaining = sum([weights[i] for i in candidates]), rest
        for i in candidates:
            extra = min(most - holding[i], max(1, remaining * weights[i] // pool), rest)
            holding[i] = holding[i] + extra
            rest = rest - extra
    return np.array([most] + holding)


def ragged_sizes(own_key, count, total, most, skew):
    if count == 2:
        one = jax.random.randint(own_key, (), max(1, total - most), min(most, total - 1) + 1)
        return jnp.stack([one, total - one])
    tallies = jnp.asarray(length_profile(count, total, most, skew), jnp.int32)
    twos = (count - 1) // 2
    source_of, receiver = tallies[1:1 + 2 * twos:2], tallies[2:2 + 2 * twos:2]
    room = jnp.minimum(source_of - 1, most - receiver)
    moved = jax.random.randint(jax.random.fold_in(own_key, 1), (twos,), 0, 1 << 20) % (room + 1)
    tallies = tallies.at[1:1 + 2 * twos:2].set(source_of - moved).at[2:2 + 2 * twos:2].set(receiver + moved)
    return tallies[jax.random.permutation(jax.random.fold_in(own_key, 2), count)]


def normal_values(own_key, dims, scale, reach, cuts=(), held_as=jnp.bfloat16):
    entries = scale * jax.random.normal(own_key, dims, jnp.float32)
    if cuts:
        entries = entries * block_scale(own_key, dims, cuts, -0.22, 0.18)
    return jnp.clip(entries, -reach, reach).astype(held_as)


def bell_draw_with(stream_key, shape, scale, limit, pieces, heavy, kind=jnp.bfloat16):
    drawn = scale * jax.random.normal(stream_key, shape, jnp.float32)
    if pieces:
        drawn = drawn * block_scale(stream_key, shape, pieces, -0.22, 0.18)
    return jnp.clip(raised(drawn, jax.random.fold_in(stream_key, 3), *heavy), -limit, limit).astype(kind)


def setup_inputs(seed: int = 0) -> dict:
    arg_keys = jax.random.split(jax.random.key(seed), 17)
    inputs = draw_inputs(jax.random.fold_in(arg_keys[16], 71), 0)
    image_ids = jnp.searchsorted(jnp.cumsum(ragged_sizes(arg_keys[1], IMAGES, TOKENS, MAXLEN, 0)), jnp.arange(TOKENS), side="right").astype(jnp.int32)
    output_gradient = bell_draw_with(arg_keys[2], (TOKENS, D), 1.0, 6.0, ((0, 32),), (0, 1, 32, 2.75), jnp.float32)
    first_norm_scale = jnp.clip(1.0 + 0.1 * jax.random.normal(arg_keys[3], (D,), jnp.float32), 0.5, 1.5)
    first_norm_bias = normal_values(arg_keys[4], (D,), 0.3, 1.5, ((0, 8),), jnp.float32)
    w_qkv = draw_w_qkv(jax.random.fold_in(arg_keys[16], 71), 0)
    bias_query = normal_values(arg_keys[6], (D,), 0.3, 1.5, ((0, 8),), jnp.float32)
    bias_value = normal_values(arg_keys[7], (D,), 0.3, 1.5, ((0, 8),), jnp.float32)
    w_output = normal_values(arg_keys[8], (D, D), (D // 64) ** -0.5, 1.75, ((0, 8),), jnp.float32)
    bias_output = normal_values(arg_keys[9], (D,), 0.3, 1.5, ((0, 8),), jnp.float32)
    second_norm_scale = jnp.clip(1.0 + 0.1 * jax.random.normal(arg_keys[10], (D,), jnp.float32), 0.5, 1.5)
    second_norm_bias = normal_values(arg_keys[11], (D,), 0.3, 1.5, ((0, 8),), jnp.float32)
    w_up = normal_values(arg_keys[12], (D, FF), D ** -0.5, 0.21875, ((0, 8),), jnp.float32)
    bias_up = normal_values(arg_keys[13], (FF,), 0.3, 1.5, ((0, 8),), jnp.float32)
    w_down = normal_values(arg_keys[14], (FF, D), FF ** -0.5, 0.109375, ((1, 8),), jnp.float32)
    bias_down = normal_values(arg_keys[15], (D,), 0.3, 1.5, ((0, 8),), jnp.float32)
    return {"inputs": inputs, "image_ids": image_ids, "output_gradient": output_gradient, "first_norm_scale": first_norm_scale, "first_norm_bias": first_norm_bias, "w_qkv": w_qkv, "bias_query": bias_query, "bias_value": bias_value, "w_output": w_output, "bias_output": bias_output, "second_norm_scale": second_norm_scale, "second_norm_bias": second_norm_bias, "w_up": w_up, "bias_up": bias_up, "w_down": w_down, "bias_down": bias_down}


HIGH = lax.Precision.HIGHEST

def matmul(left, right):
    return jnp.dot(left, right, precision=HIGH, preferred_element_type=jnp.float32)

def layer_norm_forward(rows, norm_scale, norm_bias):
    centered_input = rows - lax.optimization_barrier(jnp.mean(rows, axis=-1, keepdims=True))
    inverse_deviation = lax.rsqrt(lax.optimization_barrier(jnp.mean(centered_input * centered_input, axis=-1, keepdims=True)) + 1e-06)
    standardized = centered_input * inverse_deviation
    return (standardized * norm_scale + norm_bias, standardized, inverse_deviation)

def layer_norm_backward(upstream_gradient, standardized, inverse_deviation, norm_scale):
    scaled_values = upstream_gradient * norm_scale
    return inverse_deviation * (scaled_values - lax.optimization_barrier(jnp.mean(scaled_values, axis=-1, keepdims=True)) - standardized * lax.optimization_barrier(jnp.mean(scaled_values * standardized, axis=-1, keepdims=True)))

def gelu_parts(pre):
    cdf = 0.5 * (1.0 + jax.scipy.special.erf(pre / math.sqrt(2.0)))
    slope = cdf + pre * jnp.exp(-0.5 * pre * pre) / math.sqrt(2.0 * math.pi)
    return (pre * cdf, slope)

def heads_of(rows, heads):
    return rows.reshape(rows.shape[0], heads, -1)

def attend(q_rows, k_rows, v_rows, ids_q, ids_k, heads):
    q3 = heads_of(q_rows, heads)
    k3 = heads_of(k_rows, heads)
    v3 = heads_of(v_rows, heads)
    scale = 1.0 / math.sqrt(q3.shape[2])
    scores = jnp.einsum('qhd,khd->hqk', q3, k3, precision=HIGH) * scale
    same = (ids_q[:, None] == ids_k[None, :])[None]
    scores = jnp.where(same, scores, -1e+30)
    top = lax.optimization_barrier(jnp.max(scores, axis=-1, keepdims=True))
    weights = jnp.exp(scores - top)
    total = lax.optimization_barrier(jnp.sum(weights, axis=-1, keepdims=True))
    summed = jnp.einsum('hqk,khd->qhd', weights, v3, precision=HIGH)
    out = summed / jnp.transpose(total, (1, 0, 2))
    lse = jnp.transpose((top + jnp.log(total))[:, :, 0])
    return (out.reshape(q_rows.shape[0], -1), lse)

def probs_of(q3, k3, lse, ids_q, ids_k):
    scale = 1.0 / math.sqrt(q3.shape[2])
    scores = jnp.einsum('qhd,khd->hqk', q3, k3, precision=HIGH) * scale
    same = (ids_q[:, None] == ids_k[None, :])[None]
    return jnp.where(same, jnp.exp(scores - jnp.transpose(lse)[:, :, None]), 0.0)

def grad_queries(q_rows, g_rows, lse, delta, ids_q, k_rows, v_rows, ids_k, heads):
    q3 = heads_of(q_rows, heads)
    g3 = heads_of(g_rows, heads)
    k3 = heads_of(k_rows, heads)
    v3 = heads_of(v_rows, heads)
    probs = probs_of(q3, k3, lse, ids_q, ids_k)
    d_probs = jnp.einsum('qhd,khd->hqk', g3, v3, precision=HIGH)
    d_scores = probs * (d_probs - jnp.transpose(delta)[:, :, None])
    scale = 1.0 / math.sqrt(q3.shape[2])
    d_q = jnp.einsum('hqk,khd->qhd', d_scores, k3, precision=HIGH) * scale
    return d_q.reshape(q_rows.shape[0], -1)

def grad_keys(q_rows, g_rows, lse, delta, ids_q, k_rows, v_rows, ids_k, heads):
    q3 = heads_of(q_rows, heads)
    g3 = heads_of(g_rows, heads)
    k3 = heads_of(k_rows, heads)
    v3 = heads_of(v_rows, heads)
    probs = probs_of(q3, k3, lse, ids_q, ids_k)
    d_probs = jnp.einsum('qhd,khd->hqk', g3, v3, precision=HIGH)
    d_scores = probs * (d_probs - jnp.transpose(delta)[:, :, None])
    scale = 1.0 / math.sqrt(q3.shape[2])
    d_k = jnp.einsum('hqk,qhd->khd', d_scores, q3, precision=HIGH) * scale
    d_v = jnp.einsum('hqk,qhd->khd', probs, g3, precision=HIGH)
    return (d_k.reshape(k_rows.shape[0], -1), d_v.reshape(k_rows.shape[0], -1))

def padded(rows, width):
    return jnp.pad(rows, ((width, width),) + ((0, 0),) * (rows.ndim - 1))

def reference(inputs, image_ids, output_gradient, first_norm_scale, first_norm_bias, w_qkv, bias_query, bias_value, w_output, bias_output, second_norm_scale, second_norm_bias, w_up, bias_up, w_down, bias_down):
    width = w_output.shape[0]
    tokens = inputs.shape[0]
    block = min(512, TOK_DEV)
    count = tokens // block
    window = block + 2 * HALO
    starts = jnp.arange(count, dtype=jnp.int32) * block
    ids_one = image_ids + 1
    first_normalized, first_standardized, first_inverse_deviation = layer_norm_forward(inputs, first_norm_scale, first_norm_bias)
    proj = matmul(first_normalized, w_qkv)
    query = proj[:, :width] + bias_query
    key = proj[:, width:2 * width]
    value = proj[:, 2 * width:] + bias_value
    key_pad, value_pad, ids_pad = (padded(key, HALO), padded(value, HALO), padded(ids_one, HALO))

    def forward_block(start):
        q_rows = lax.dynamic_slice_in_dim(query, start, block)
        ids_q = lax.dynamic_slice_in_dim(ids_one, start, block)
        k_rows = lax.dynamic_slice_in_dim(key_pad, start, window)
        v_rows = lax.dynamic_slice_in_dim(value_pad, start, window)
        ids_k = lax.dynamic_slice_in_dim(ids_pad, start, window)
        return attend(q_rows, k_rows, v_rows, ids_q, ids_k, HEADS)
    attended, lse = lax.map(forward_block, starts)
    attended = attended.reshape(tokens, width)
    lse = lse.reshape(tokens, HEADS)
    middle_state = inputs + matmul(attended, w_output) + bias_output
    second_normalized, second_standardized, second_inverse_deviation = layer_norm_forward(middle_state, second_norm_scale, second_norm_bias)
    pre = matmul(second_normalized, w_up) + bias_up
    act, slope = gelu_parts(pre)
    outputs = middle_state + matmul(act, w_down) + bias_down
    grad_bias_down = lax.optimization_barrier(jnp.sum(output_gradient, axis=0))
    grad_w_down = matmul(act.T, output_gradient)
    d_pre = matmul(output_gradient, w_down.T) * slope
    grad_bias_up = lax.optimization_barrier(jnp.sum(d_pre, axis=0))
    grad_w_up = matmul(second_normalized.T, d_pre)
    gradient_second_normalized = matmul(d_pre, w_up.T)
    gradient_second_norm_scale = lax.optimization_barrier(jnp.sum(gradient_second_normalized * second_standardized, axis=0))
    grad_norm2_bias = lax.optimization_barrier(jnp.sum(gradient_second_normalized, axis=0))
    gradient_middle = output_gradient + layer_norm_backward(gradient_second_normalized, second_standardized, second_inverse_deviation, second_norm_scale)
    grad_bias_output = lax.optimization_barrier(jnp.sum(gradient_middle, axis=0))
    grad_w_output = matmul(attended.T, gradient_middle)
    d_attended = matmul(gradient_middle, w_output.T)
    delta = lax.optimization_barrier(jnp.sum(heads_of(d_attended * attended, HEADS), axis=-1))
    query_pad, grad_pad = (padded(query, HALO), padded(d_attended, HALO))
    lse_pad, delta_pad = (padded(lse, HALO), padded(delta, HALO))

    def query_block(start):
        return grad_queries(lax.dynamic_slice_in_dim(query, start, block), lax.dynamic_slice_in_dim(d_attended, start, block), lax.dynamic_slice_in_dim(lse, start, block), lax.dynamic_slice_in_dim(delta, start, block), lax.dynamic_slice_in_dim(ids_one, start, block), lax.dynamic_slice_in_dim(key_pad, start, window), lax.dynamic_slice_in_dim(value_pad, start, window), lax.dynamic_slice_in_dim(ids_pad, start, window), HEADS)

    def key_block(start):
        return grad_keys(lax.dynamic_slice_in_dim(query_pad, start, window), lax.dynamic_slice_in_dim(grad_pad, start, window), lax.dynamic_slice_in_dim(lse_pad, start, window), lax.dynamic_slice_in_dim(delta_pad, start, window), lax.dynamic_slice_in_dim(ids_pad, start, window), lax.dynamic_slice_in_dim(key, start, block), lax.dynamic_slice_in_dim(value, start, block), lax.dynamic_slice_in_dim(ids_one, start, block), HEADS)
    d_query = lax.map(query_block, starts).reshape(tokens, width)
    d_key, d_value = lax.map(key_block, starts)
    d_key = d_key.reshape(tokens, width)
    d_value = d_value.reshape(tokens, width)
    d_proj = jnp.concatenate([d_query, d_key, d_value], axis=1)
    grad_w_qkv = matmul(first_normalized.T, d_proj)
    grad_bias_query = lax.optimization_barrier(jnp.sum(d_query, axis=0))
    grad_bias_value = lax.optimization_barrier(jnp.sum(d_value, axis=0))
    gradient_first_normalized = matmul(d_proj, w_qkv.T)
    gradient_first_norm_scale = lax.optimization_barrier(jnp.sum(gradient_first_normalized * first_standardized, axis=0))
    grad_norm1_bias = lax.optimization_barrier(jnp.sum(gradient_first_normalized, axis=0))
    gradient_of_input = gradient_middle + layer_norm_backward(gradient_first_normalized, first_standardized, first_inverse_deviation, first_norm_scale)
    return (outputs, gradient_of_input, gradient_first_norm_scale, grad_norm1_bias, grad_w_qkv, grad_bias_query, grad_bias_value, grad_w_output, grad_bias_output, gradient_second_norm_scale, grad_norm2_bias, grad_w_up, grad_bias_up, grad_w_down, grad_bias_down)
```

```python
import math

import jax
import jax.numpy as jnp
from jax import lax
from jax.experimental import pallas as pl
from jax.experimental.pallas import tpu as pltpu
from jax.sharding import PartitionSpec as P

HEADS = 12
HEAD = 64
REACH = 200
PAD = 8
HIGH = lax.Precision.HIGH
EXACT = lax.Precision.HIGHEST


def matmul(left, right, dims=((1,), (0,))):
    return lax.dot_general(
        left, right, (dims, ((), ())), precision=HIGH, preferred_element_type=jnp.float32
    )


def layer_norm_forward(rows, norm_scale, norm_bias):
    centered_input = rows - jnp.mean(rows, axis=-1, keepdims=True)
    inverse_deviation = lax.rsqrt(
        jnp.mean(centered_input * centered_input, axis=-1, keepdims=True) + 1e-06
    )
    standardized = centered_input * inverse_deviation
    return (standardized * norm_scale + norm_bias, standardized, inverse_deviation)


def layer_norm_backward(upstream_gradient, standardized, inverse_deviation, norm_scale):
    scaled_values = upstream_gradient * norm_scale
    return inverse_deviation * (
        scaled_values
        - jnp.mean(scaled_values, axis=-1, keepdims=True)
        - standardized * jnp.mean(scaled_values * standardized, axis=-1, keepdims=True)
    )


def gelu_parts(pre):
    cdf = 0.5 * (1.0 + jax.scipy.special.erf(pre / math.sqrt(2.0)))
    slope = cdf + pre * jnp.exp(-0.5 * pre * pre) / math.sqrt(2.0 * math.pi)
    return (pre * cdf, slope)


def halves(x):
    hi = x.astype(jnp.bfloat16)
    lo = (x - hi.astype(jnp.float32)).astype(jnp.bfloat16)
    return hi, lo


def left3(x):
    hi, lo = halves(x)
    return jnp.concatenate([hi, hi, lo], axis=1)


def right3(x):
    hi, lo = halves(x)
    return jnp.concatenate([hi, lo, hi], axis=1)


def dot_nt(a, b):
    return lax.dot_general(a, b, (((1,), (1,)), ((), ())), preferred_element_type=jnp.float32)


def weighted(p, x):
    hi, lo = halves(p)
    xh, xl = halves(x)
    both = jnp.dot(hi, jnp.concatenate([xh, xl], axis=1), preferred_element_type=jnp.float32)
    return both[:, :HEAD] + both[:, HEAD:] + jnp.dot(lo, xh, preferred_element_type=jnp.float32)


def forward_kernel(q_ref, k_ref, v_ref, idc_ref, idr_ref, out_ref, lse_ref):
    same = idc_ref[0] == idr_ref[0]
    outs, lses = [], []
    for h in range(2):
        cols = slice(h * HEAD, (h + 1) * HEAD)
        q = q_ref[0][:, cols] * (1.0 / math.sqrt(HEAD))
        s = dot_nt(left3(q), right3(k_ref[0][:, cols]))
        s = jnp.where(same, s, -1e30)
        top = jnp.max(s, axis=1, keepdims=True)
        w = jnp.exp(s - top)
        total = jnp.sum(w, axis=1, keepdims=True)
        outs.append(weighted(w, v_ref[0][:, cols]) / total)
        lses.append(jnp.broadcast_to(top + jnp.log(total), (q.shape[0], HEAD)))
    out_ref[0] = jnp.concatenate(outs, axis=1)
    lse_ref[0] = jnp.concatenate(lses, axis=1)


def query_kernel(q_ref, k_ref, v_ref, g_ref, out_ref, lse_ref, idc_ref, idr_ref, dq_ref):
    same = idc_ref[0] == idr_ref[0]
    scale = 1.0 / math.sqrt(HEAD)
    outs = []
    for h in range(2):
        cols = slice(h * HEAD, (h + 1) * HEAD)
        q, k = q_ref[0][:, cols] * scale, k_ref[0][:, cols]
        g = g_ref[0][:, cols]
        lse = lse_ref[0][:, h * HEAD : h * HEAD + 1]
        delta = jnp.sum(g * out_ref[0][:, cols], axis=1, keepdims=True)
        s = dot_nt(left3(q), right3(k))
        p = jnp.exp(jnp.where(same, s - lse, -1e30))
        d_p = dot_nt(left3(g), right3(v_ref[0][:, cols]))
        outs.append(weighted(p * (d_p - delta), k) * scale)
    dq_ref[0] = jnp.concatenate(outs, axis=1)


def key_kernel(q_ref, g_ref, lse_ref, delta_ref, k_ref, v_ref, idc_ref, idr_ref, dk_ref, dv_ref):
    same = idc_ref[0] == idr_ref[0]
    scale = 1.0 / math.sqrt(HEAD)
    d_k, d_v = [], []
    for h in range(2):
        cols = slice(h * HEAD, (h + 1) * HEAD)
        q = q_ref[0][:, cols] * scale
        g = g_ref[0][:, cols]
        row = 2 * pl.program_id(1) + h
        lse = lse_ref[0, pl.ds(row, 1), :]
        delta = delta_ref[0, pl.ds(row, 1), :]
        s = dot_nt(left3(k_ref[0][:, cols]), right3(q))
        p = jnp.exp(jnp.where(same, s - lse, -1e30))
        d_p = dot_nt(left3(v_ref[0][:, cols]), right3(g))
        d_v.append(weighted(p, g))
        d_k.append(weighted(p * (d_p - delta), q))
    dk_ref[0] = jnp.concatenate(d_k, axis=1)
    dv_ref[0] = jnp.concatenate(d_v, axis=1)


def head_block(rows, first=0):
    return pl.BlockSpec((1, rows, 2 * HEAD), lambda b, h: (b, 0, first + h))


def whole_block(*shape):
    return pl.BlockSpec((1,) + shape, lambda b, h: (b, 0, 0))


def attention_forward(proj, ids_col, ids_row, own, width):
    blocks, ext, _ = proj.shape
    pairs = width // (2 * HEAD)
    return pl.pallas_call(
        forward_kernel,
        grid=(blocks, pairs),
        in_specs=[
            head_block(own),
            head_block(ext, pairs),
            head_block(ext, 2 * pairs),
            whole_block(own, 1),
            whole_block(1, ext),
        ],
        out_specs=[head_block(own), head_block(own)],
        out_shape=[jax.ShapeDtypeStruct((blocks, own, width), jnp.float32)] * 2,
        name="attend",
    )(proj, proj, proj, ids_col, ids_row)


def attention_queries(proj, grads, out, lse, ids_col, ids_row, own, width):
    blocks, ext, _ = proj.shape
    pairs = width // (2 * HEAD)
    return pl.pallas_call(
        query_kernel,
        grid=(blocks, pairs),
        in_specs=[
            head_block(own),
            head_block(ext, pairs),
            head_block(ext, 2 * pairs),
            head_block(own),
            head_block(own),
            head_block(own),
            whole_block(own, 1),
            whole_block(1, ext),
        ],
        out_specs=head_block(own),
        out_shape=jax.ShapeDtypeStruct((blocks, own, width), jnp.float32),
        name="grad_queries",
    )(proj, proj, proj, grads, out, lse, ids_col, ids_row)


def attention_keys(proj, grads, lse_rows, delta_rows, ids_col, ids_row, own, width):
    blocks, ext, _ = proj.shape
    pairs = width // (2 * HEAD)
    rows = lse_rows.shape[1]
    return pl.pallas_call(
        key_kernel,
        grid=(blocks, pairs),
        in_specs=[
            head_block(ext),
            head_block(ext),
            whole_block(rows, ext),
            whole_block(rows, ext),
            head_block(own, pairs),
            head_block(own, 2 * pairs),
            whole_block(own, 1),
            whole_block(1, ext),
        ],
        out_specs=[head_block(own), head_block(own)],
        out_shape=[jax.ShapeDtypeStruct((blocks, own, width), jnp.float32)] * 2,
        name="grad_keys",
    )(proj, grads, lse_rows, delta_rows, proj, proj, ids_col, ids_row)


def flip(x, bit):
    count = lax.axis_size("shard")
    return lax.ppermute(x, "shard", [(i, i ^ bit) for i in range(count)])


def partner(x):
    return flip(x, 1)


def gathered_pieces(piece, chips):
    if chips == 4:
        half = piece.shape[0] // 2
        from_x, from_y = flip(piece, 2), flip(piece, 4)
        upper, lower = flip(from_x[:half], 4), flip(from_y[half:], 2)
        return [(0, None, piece), (1, None, from_x), (2, None, from_y), (3, 0, upper), (3, 1, lower)]
    pieces = {0: piece}
    step = 1
    while step < chips:
        joined = jnp.concatenate([pieces[i] for i in range(step)], axis=0)
        other = flip(joined, 2 * step)
        rows = piece.shape[0]
        for i in range(step):
            pieces[step + i] = other[i * rows : (i + 1) * rows]
        step *= 2
    return [(i, None, p) for i, p in pieces.items()]


def gather_rows(piece, chips, chip, rows):
    per = piece.shape[0] // 2
    extra = per - rows
    main = jnp.zeros((2 * chips * rows, piece.shape[1]), piece.dtype)
    rest = jnp.zeros((2 * chips * extra, piece.shape[1]), piece.dtype) if extra else None
    for which, part, values in gathered_pieces(piece, chips):
        at = chip ^ which
        for j in (0, 1) if part is None else (part,):
            base = j * per if part is None else 0
            shard = 2 * at + j
            main = lax.dynamic_update_slice(main, values[base : base + rows], (shard * rows, 0))
            if extra:
                rest = lax.dynamic_update_slice(
                    rest, values[base + rows : base + per], (shard * extra, 0)
                )
    return main, rest


def scatter_rows(full, chips, chip):
    n = full.shape[0] // chips

    def rows(which, start=0, count=n):
        return lax.dynamic_slice_in_dim(full, (chip ^ which) * n + start, count, axis=0)

    if chips == 4:
        half = n // 2
        via_x = flip(rows(3, 0, half), 2)
        via_y = flip(rows(3, half, half), 4)
        to_y = flip(jnp.concatenate([rows(2, 0, half) + via_x, rows(2, half, half)]), 4)
        to_x = flip(jnp.concatenate([rows(1, 0, half), rows(1, half, half) + via_y]), 2)
        return rows(0) + to_y + to_x
    held = [rows(i) for i in range(chips)]
    step = chips // 2
    while step:
        other = flip(jnp.concatenate(held[step:], axis=0), 2 * step)
        held = [held[i] + other[i * n : (i + 1) * n] for i in range(step)]
        step //= 2
    return held[0]


def halo_moves(shards, reps):
    own_prev, other_prev, own_next, other_next = [], [], [], []
    for s in range(shards):
        for r in range(reps):
            here = s * reps + r
            if r > 0:
                own_prev.append((here - 1, here))
                other_prev.append((here - 1, here))
            else:
                source = s if s % 2 else s - 2
                if source >= 0:
                    own_prev.append((source * reps + reps - 1, here))
                source = s - 2 if s % 2 else s
                if source >= 0:
                    other_prev.append((source * reps + reps - 1, here))
            if r < reps - 1:
                own_next.append((here + 1, here))
                other_next.append((here + 1, here))
            else:
                source = s + 2 if s % 2 else s
                if source < shards:
                    own_next.append((source * reps, here))
                source = s if s % 2 else s + 2
                if source < shards:
                    other_next.append((source * reps, here))
    return own_prev, other_prev, own_next, other_next


def ordered(mine, theirs, odd, axis):
    size = mine.shape[axis]
    shape = list(mine.shape)
    shape[axis] = 2 * size
    both = jnp.zeros(tuple(shape), mine.dtype)
    both = lax.dynamic_update_slice_in_dim(both, mine, odd * size, axis)
    return lax.dynamic_update_slice_in_dim(both, theirs, (1 - odd) * size, axis)


def swap_halves(x):
    n = x.shape[0] // 2
    return jnp.concatenate([x[n:], x[:n]], axis=0)


def pair_sum(x):
    return x + swap_halves(partner(x))


def pick(x, index, size, axis):
    return lax.dynamic_slice_in_dim(x, index * size, size, axis)


def per_device(
    inputs,
    image_ids,
    output_gradient,
    first_norm_scale,
    first_norm_bias,
    w_qkv,
    bias_query,
    bias_value,
    w_output,
    bias_output,
    second_norm_scale,
    second_norm_bias,
    w_up,
    bias_up,
    w_down,
    bias_down,
):
    shards, reps = lax.axis_size("shard"), lax.axis_size("rep")
    chips = shards // 2
    shard, rep = lax.axis_index("shard"), lax.axis_index("rep")
    chip, odd = shard // 2, shard % 2
    axes = ("shard", "rep")
    own, width = inputs.shape
    rows = w_qkv.shape[0]
    mine = width // 2
    hidden = w_up.shape[1] // 2
    ext = own + 2 * REACH

    ids = (image_ids + 1).astype(jnp.float32)

    def with_ids(x, x_ids):
        line = jnp.pad(x_ids[None], ((0, PAD - 1), (0, width - x_ids.shape[0])))
        return jnp.concatenate([x, line], axis=0)

    forward = [(i, i + 1) for i in range(shards * reps - 1)]
    backward = [(b, a) for a, b in forward]
    low = lax.ppermute(with_ids(inputs[own - REACH :], ids[own - REACH :]), axes, forward)
    high = lax.ppermute(with_ids(inputs[:REACH], ids[:REACH]), axes, backward)
    ids_ext = jnp.concatenate([ids, low[REACH, :REACH], high[REACH, :REACH]])
    x_ext = jnp.concatenate([inputs, low[:REACH], high[:REACH]], axis=0)
    other_ext = partner(with_ids(x_ext, ids_ext))
    ids_two = jnp.stack([ids_ext, other_ext[ext, :ext]])
    ids_col, ids_row = ids_two[:, :own, None], ids_two[:, None, :]
    tokens = jnp.concatenate([x_ext, other_ext[:ext]], axis=0)
    g_two = jnp.concatenate([output_gradient, partner(output_gradient)], axis=0)

    small = jnp.concatenate(
        [
            first_norm_scale,
            first_norm_bias,
            second_norm_scale,
            second_norm_bias,
            bias_output,
            bias_down,
            bias_query,
            bias_value,
            bias_up,
        ]
    )
    lead = 3 * mine
    small = jnp.pad(small, (0, -small.shape[0] % lead)).reshape(-1, lead)
    small = jnp.pad(small, ((0, -small.shape[0] % PAD), (0, 0)))
    extra = small.shape[0]
    by_half = w_qkv.reshape(rows, 3, 2, mine)

    def qkv_half(which):
        return pick(by_half, which, 1, 2).reshape(rows, lead)

    first = ordered(
        jnp.concatenate([qkv_half(odd), small]),
        partner(jnp.concatenate([qkv_half(1 - odd), small])),
        odd,
        0,
    )
    wqkv, gathered_small = gather_rows(first, chips, chip, rows)

    w_down_t = w_down.T

    def second_half(which):
        return jnp.concatenate([pick(w_output, which, mine, 1), pick(w_up, which, hidden, 1)], axis=1)

    second = ordered(second_half(odd), partner(second_half(1 - odd)), odd, 0)
    third = ordered(
        pick(w_down_t, odd, hidden, 1), partner(pick(w_down_t, 1 - odd, hidden, 1)), odd, 0
    )
    out_up, _ = gather_rows(second, chips, chip, rows)
    wup = out_up[:, mine:]
    out_cols = out_up[:, :mine]
    wout = ordered(
        pick(out_cols, odd, mine, 0), partner(pick(out_cols, 1 - odd, mine, 0)), odd, 1
    )
    wdown_t, _ = gather_rows(third, chips, chip, rows)

    table = gathered_small.reshape(shards, extra * lead)

    def vector(start, size):
        return table[:, start : start + size].reshape(shards * size)

    first_scale, first_bias, second_scale, second_bias, bout, bdown, bq, bv = (
        vector(i * rows, rows) for i in range(8)
    )
    bup = pick(vector(8 * rows, bias_up.shape[0]), odd, hidden, 0)
    shift = jnp.concatenate(
        [pick(bq, odd, mine, 0), jnp.zeros((mine,), jnp.float32), pick(bv, odd, mine, 0)]
    )

    first_normalized, first_standardized, first_inverse_deviation = layer_norm_forward(
        tokens, first_scale, first_bias
    )
    proj = (matmul(first_normalized, wqkv) + shift).reshape(2, ext, lead)
    attended, lse = attention_forward(proj, ids_col, ids_row, own, mine)
    out_rows = attended.reshape(2 * own, mine)
    x_two = jnp.concatenate([tokens[:own], tokens[ext : ext + own]], axis=0)
    middle_state = x_two + pair_sum(matmul(out_rows, wout)) + bout

    second_normalized, second_standardized, second_inverse_deviation = layer_norm_forward(
        middle_state, second_scale, second_bias
    )
    pre = matmul(second_normalized, wup) + bup
    act, slope = gelu_parts(pre)
    down = matmul(act, wdown_t, ((1,), (1,)))
    outputs = middle_state[:own] + (down[:own] + partner(down[own:])) + bdown
    grad_down_t = matmul(g_two, act, ((0,), (0,)))
    d_pre = matmul(g_two, wdown_t) * slope
    grad_bias_up = jnp.sum(d_pre, axis=0)
    grad_up = matmul(second_normalized, d_pre, ((0,), (0,)))
    d_second = pair_sum(matmul(d_pre, wup, ((1,), (1,))))
    gradient_middle = g_two + layer_norm_backward(
        d_second, second_standardized, second_inverse_deviation, second_scale
    )

    d_attended = matmul(gradient_middle, wout, ((1,), (1,)))
    grad_out = matmul(out_rows, gradient_middle, ((0,), (0,)))
    heads = mine // HEAD
    lse_rows = jnp.swapaxes(lse.reshape(2, own, heads, HEAD)[..., 0], 1, 2)
    member = (
        jnp.arange(mine)[None, :] // HEAD == jnp.arange(heads)[:, None]
    ).astype(jnp.float32)
    delta_rows = lax.dot_general(
        member,
        d_attended * out_rows,
        (((1,), (1,)), ((), ())),
        precision=EXACT,
        preferred_element_type=jnp.float32,
    )
    delta_rows = jnp.swapaxes(delta_rows.reshape(heads, 2, own), 0, 1)
    grads = d_attended.reshape(2, own, mine)
    stats = jnp.concatenate([lse_rows, delta_rows], axis=1)
    lines = -2 * heads % PAD + 2 * heads

    def edge(start):
        s = jnp.pad(
            stats[:, :, start : start + REACH],
            ((0, 0), (0, lines - 2 * heads), (0, mine - REACH)),
        )
        return jnp.concatenate([grads[:, start : start + REACH], s], axis=1)

    own_prev, other_prev, own_next, other_next = halo_moves(shards, reps)
    tail, head = edge(own - REACH), edge(0)
    at_end = (rep == reps - 1).astype(jnp.int32)
    at_start = (rep == 0).astype(jnp.int32)

    def block(x, index):
        return lax.dynamic_index_in_dim(x, index, 0, keepdims=False)

    prev = [
        lax.ppermute(block(tail, at_end), axes, own_prev),
        lax.ppermute(block(tail, 1 - at_end), axes, other_prev),
    ]
    following = [
        lax.ppermute(block(head, at_start), axes, own_next),
        lax.ppermute(block(head, 1 - at_start), axes, other_next),
    ]
    d_query = attention_queries(proj, grads, attended, lse, ids_col, ids_row, own, mine)
    grads_ext = jnp.stack(
        [
            jnp.concatenate([grads[b], prev[b][:REACH], following[b][:REACH]], axis=0)
            for b in range(2)
        ]
    )
    stats_ext = jnp.stack(
        [
            jnp.concatenate(
                [
                    stats[b],
                    prev[b][REACH : REACH + 2 * heads, :REACH],
                    following[b][REACH : REACH + 2 * heads, :REACH],
                ],
                axis=1,
            )
            for b in range(2)
        ]
    )
    d_key, d_value = attention_keys(
        proj, grads_ext, stats_ext[:, :heads], stats_ext[:, heads:], ids_col, ids_row, own, mine
    )
    d_proj = jnp.concatenate([d_query, d_key, d_value], axis=2).reshape(2 * own, lead)
    normalized_two = jnp.concatenate(
        [first_normalized[:own], first_normalized[ext : ext + own]], axis=0
    )
    grad_qkv = matmul(normalized_two, d_proj, ((0,), (0,)))
    d_first = matmul(d_proj, wqkv, ((1,), (1,)))
    d_first = d_first[:own] + partner(d_first[own:])
    gradient_of_input = gradient_middle[:own] + layer_norm_backward(
        d_first, first_standardized[:own], first_inverse_deviation[:own], first_scale
    )

    sums = jnp.sum(d_proj, axis=0)

    def spread(half):
        full = jnp.zeros((2 * half.shape[0],), jnp.float32)
        return lax.dynamic_update_slice_in_dim(full, half, odd * half.shape[0], 0)

    small_sums = [
        jnp.sum(d_first * first_standardized[:own], axis=0),
        jnp.sum(d_first, axis=0),
        jnp.sum(d_second[:own] * second_standardized[:own], axis=0),
        jnp.sum(d_second[:own], axis=0),
        jnp.sum(gradient_middle[:own], axis=0),
        jnp.sum(output_gradient, axis=0),
        spread(sums[:mine]),
        spread(sums[2 * mine :]),
        spread(grad_bias_up),
    ]
    table = jnp.concatenate([v.reshape(shards, -1) for v in small_sums], axis=1)
    table = jnp.pad(table, ((0, 0), (0, extra * lead - table.shape[1])))
    table = table.reshape(shards, extra, lead)
    last = jnp.concatenate([grad_qkv.reshape(shards, rows, lead), table], axis=1)
    last = last.reshape(shards * (rows + extra), lead)

    crossed = partner(pick(grad_out, 1 - odd, mine, 1))
    grad_out = ordered(pick(grad_out, odd, mine, 1), crossed, odd, 0)
    middle = jnp.concatenate([grad_out, grad_up], axis=1)

    def finish(full):
        kept = scatter_rows(full, chips, chip)
        n = kept.shape[0] // 2
        return pick(kept, odd, n, 0), partner(pick(kept, 1 - odd, n, 0))

    down_mine, down_theirs = finish(grad_down_t)
    middle_mine, middle_theirs = finish(middle)
    last_mine, last_theirs = finish(last)

    total_down = lax.psum(ordered(down_mine, down_theirs, odd, 1), "rep")
    total_middle = lax.psum(
        jnp.concatenate(
            [
                ordered(middle_mine[:, :mine], middle_theirs[:, :mine], odd, 1),
                ordered(middle_mine[:, mine:], middle_theirs[:, mine:], odd, 1),
            ],
            axis=1,
        ),
        "rep",
    )
    small_total = last_mine[rows:] + last_theirs[rows:]
    qkv_total = ordered(
        last_mine[:rows].reshape(rows, 3, mine), last_theirs[:rows].reshape(rows, 3, mine), odd, 2
    ).reshape(rows, 2 * lead)
    qkv_total, small_total = lax.psum((qkv_total, small_total), "rep")
    small_total = small_total.reshape(-1)
    small_out = [small_total[i * rows : (i + 1) * rows] for i in range(8)]
    up_bias_out = small_total[8 * rows : 8 * rows + bias_up.shape[0]]
    return (
        outputs,
        gradient_of_input,
        small_out[0],
        small_out[1],
        qkv_total,
        small_out[6],
        small_out[7],
        total_middle[:, :width],
        small_out[4],
        small_out[2],
        small_out[3],
        total_middle[:, width:],
        up_bias_out,
        total_down.T,
        small_out[5],
    )


def solution(mesh):
    placed = (
        P(("shard", "rep"), None),
        P(("shard", "rep")),
        P(("shard", "rep"), None),
        P("shard"),
        P("shard"),
        P("shard", None),
        P("shard"),
        P("shard"),
        P("shard", None),
        P("shard"),
        P("shard"),
        P("shard"),
        P("shard", None),
        P("shard"),
        P(None, "shard"),
        P("shard"),
    )
    return jax.shard_map(
        per_device,
        mesh=mesh,
        in_specs=placed,
        out_specs=(
            P(("shard", "rep"), None),
            P(("shard", "rep"), None),
            P("shard"),
            P("shard"),
            P("shard", None),
            P("shard"),
            P("shard"),
            P("shard", None),
            P("shard"),
            P("shard"),
            P("shard"),
            P("shard", None),
            P("shard"),
            P(None, "shard"),
            P("shard"),
        ),
        check_vma=False,
    )
```

```python
import math

import jax
import jax.numpy as jnp
from jax import lax
from jax.experimental import pallas as pl
from jax.experimental.pallas import tpu as pltpu
from jax.sharding import PartitionSpec as P


HEAD = 64
REACH = 200
PAD = 8
HIGH = lax.Precision.HIGH
EXACT = lax.Precision.HIGHEST


def matmul(left, right, dims=((1,), (0,))):
    return lax.dot_general(
        left, right, (dims, ((), ())), precision=HIGH, preferred_element_type=jnp.float32
    )


def layer_norm_forward(rows, norm_scale, norm_bias):
    centered_input = rows - jnp.mean(rows, axis=-1, keepdims=True)
    inverse_deviation = lax.rsqrt(
        jnp.mean(centered_input * centered_input, axis=-1, keepdims=True) + 1e-06
    )
    standardized = centered_input * inverse_deviation
    return (standardized * norm_scale + norm_bias, standardized, inverse_deviation)


def layer_norm_backward(upstream_gradient, standardized, inverse_deviation, norm_scale):
    scaled_values = upstream_gradient * norm_scale
    return inverse_deviation * (
        scaled_values
        - jnp.mean(scaled_values, axis=-1, keepdims=True)
        - standardized * jnp.mean(scaled_values * standardized, axis=-1, keepdims=True)
    )


def gelu_parts(pre):
    cdf = 0.5 * (1.0 + jax.scipy.special.erf(pre / math.sqrt(2.0)))
    slope = cdf + pre * jnp.exp(-0.5 * pre * pre) / math.sqrt(2.0 * math.pi)
    return (pre * cdf, slope)


def halves(x):
    hi = x.astype(jnp.bfloat16)
    lo = (x - hi.astype(jnp.float32)).astype(jnp.bfloat16)
    return hi, lo


def left3(x):
    hi, lo = halves(x)
    return jnp.concatenate([hi, hi, lo], axis=1)


def right3(x):
    hi, lo = halves(x)
    return jnp.concatenate([hi, lo, hi], axis=1)


def dot_nt(a, b):
    return lax.dot_general(a, b, (((1,), (1,)), ((), ())), preferred_element_type=jnp.float32)


def weighted(p, x):
    hi, lo = halves(p)
    xh, xl = halves(x)
    both = jnp.dot(hi, jnp.concatenate([xh, xl], axis=1), preferred_element_type=jnp.float32)
    return both[:, :HEAD] + both[:, HEAD:] + jnp.dot(lo, xh, preferred_element_type=jnp.float32)


def forward_kernel(q_ref, k_ref, v_ref, idc_ref, idr_ref, out_ref, lse_ref):
    same = idc_ref[0] == idr_ref[0]
    outs, lses = [], []
    for h in range(2):
        cols = slice(h * HEAD, (h + 1) * HEAD)
        q = q_ref[0][:, cols] * (1.0 / math.sqrt(HEAD))
        s = dot_nt(left3(q), right3(k_ref[0][:, cols]))
        s = jnp.where(same, s, -1e30)
        top = jnp.max(s, axis=1, keepdims=True)
        w = jnp.exp(s - top)
        total = jnp.sum(w, axis=1, keepdims=True)
        outs.append(weighted(w, v_ref[0][:, cols]) / total)
        lses.append(jnp.broadcast_to(top + jnp.log(total), (q.shape[0], HEAD)))
    out_ref[0] = jnp.concatenate(outs, axis=1)
    lse_ref[0] = jnp.concatenate(lses, axis=1)


def query_kernel(q_ref, k_ref, v_ref, g_ref, out_ref, lse_ref, idc_ref, idr_ref, dq_ref):
    same = idc_ref[0] == idr_ref[0]
    scale = 1.0 / math.sqrt(HEAD)
    outs = []
    for h in range(2):
        cols = slice(h * HEAD, (h + 1) * HEAD)
        q, k = q_ref[0][:, cols] * scale, k_ref[0][:, cols]
        g = g_ref[0][:, cols]
        lse = lse_ref[0][:, h * HEAD : h * HEAD + 1]
        delta = jnp.sum(g * out_ref[0][:, cols], axis=1, keepdims=True)
        s = dot_nt(left3(q), right3(k))
        p = jnp.exp(jnp.where(same, s - lse, -1e30))
        d_p = dot_nt(left3(g), right3(v_ref[0][:, cols]))
        outs.append(weighted(p * (d_p - delta), k) * scale)
    dq_ref[0] = jnp.concatenate(outs, axis=1)


def key_kernel(q_ref, g_ref, lse_ref, delta_ref, k_ref, v_ref, idc_ref, idr_ref, dk_ref, dv_ref):
    same = idc_ref[0] == idr_ref[0]
    scale = 1.0 / math.sqrt(HEAD)
    d_k, d_v = [], []
    for h in range(2):
        cols = slice(h * HEAD, (h + 1) * HEAD)
        q = q_ref[0][:, cols] * scale
        g = g_ref[0][:, cols]
        row = 2 * pl.program_id(1) + h
        lse = lse_ref[0, pl.ds(row, 1), :]
        delta = delta_ref[0, pl.ds(row, 1), :]
        s = dot_nt(left3(k_ref[0][:, cols]), right3(q))
        p = jnp.exp(jnp.where(same, s - lse, -1e30))
        d_p = dot_nt(left3(v_ref[0][:, cols]), right3(g))
        d_v.append(weighted(p, g))
        d_k.append(weighted(p * (d_p - delta), q))
    dk_ref[0] = jnp.concatenate(d_k, axis=1)
    dv_ref[0] = jnp.concatenate(d_v, axis=1)


def head_block(rows, first=0):
    return pl.BlockSpec((1, rows, 2 * HEAD), lambda b, h: (b, 0, first + h))


def whole_block(*shape):
    return pl.BlockSpec((1,) + shape, lambda b, h: (b, 0, 0))


def attention_forward(proj, ids_col, ids_row, own, width):
    blocks, ext, _ = proj.shape
    pairs = width // (2 * HEAD)
    return pl.pallas_call(
        forward_kernel,
        grid=(blocks, pairs),
        in_specs=[
            head_block(own),
            head_block(ext, pairs),
            head_block(ext, 2 * pairs),
            whole_block(own, 1),
            whole_block(1, ext),
        ],
        out_specs=[head_block(own), head_block(own)],
        out_shape=[jax.ShapeDtypeStruct((blocks, own, width), jnp.float32)] * 2,
        name="attend",
    )(proj, proj, proj, ids_col, ids_row)


def attention_queries(proj, grads, out, lse, ids_col, ids_row, own, width):
    blocks, ext, _ = proj.shape
    pairs = width // (2 * HEAD)
    return pl.pallas_call(
        query_kernel,
        grid=(blocks, pairs),
        in_specs=[
            head_block(own),
            head_block(ext, pairs),
            head_block(ext, 2 * pairs),
            head_block(own),
            head_block(own),
            head_block(own),
            whole_block(own, 1),
            whole_block(1, ext),
        ],
        out_specs=head_block(own),
        out_shape=jax.ShapeDtypeStruct((blocks, own, width), jnp.float32),
        name="grad_queries",
    )(proj, proj, proj, grads, out, lse, ids_col, ids_row)


def attention_keys(proj, grads, lse_rows, delta_rows, ids_col, ids_row, own, width):
    blocks, ext, _ = proj.shape
    pairs = width // (2 * HEAD)
    rows = lse_rows.shape[1]
    return pl.pallas_call(
        key_kernel,
        grid=(blocks, pairs),
        in_specs=[
            head_block(ext),
            head_block(ext),
            whole_block(rows, ext),
            whole_block(rows, ext),
            head_block(own, pairs),
            head_block(own, 2 * pairs),
            whole_block(own, 1),
            whole_block(1, ext),
        ],
        out_specs=[head_block(own), head_block(own)],
        out_shape=[jax.ShapeDtypeStruct((blocks, own, width), jnp.float32)] * 2,
        name="grad_keys",
    )(proj, grads, lse_rows, delta_rows, proj, proj, ids_col, ids_row)


def flip(x, bit):
    count = lax.axis_size("shard")
    return lax.ppermute(x, "shard", [(i, i ^ bit) for i in range(count)])


def partner(x):
    return flip(x, 1)


def gathered_pieces(piece, chips, after=None):
    rows = piece.shape[0]
    if after is not None:
        piece, after = lax.optimization_barrier((piece, after))
    if chips == 4:
        half = rows // 2
        from_x, from_y = flip(piece, 2), flip(piece, 4)
        upper, lower = flip(from_x[:half], 4), flip(from_y[half:], 2)
        held = [
            (piece, [(0, 0, 0, rows)]),
            (from_x, [(0, 1, 0, rows)]),
            (from_y, [(0, 2, 0, rows)]),
            (upper, [(0, 3, 0, half)]),
            (lower, [(0, 3, half, half)]),
        ]
        return held, (upper, lower)
    held = [(piece, [(0, 0, 0, rows)])]
    step = 1
    while step < chips:
        joined = jnp.concatenate([x for x, _ in held], axis=0)
        spans = [(i * rows, step + i, 0, rows) for i in range(step)]
        held.append((flip(joined, 2 * step), spans))
        step *= 2
    return held, held[-1][0]


def assemble(held, chips, place, plans):
    copies = []
    for index, (_, spans) in enumerate(held):
        for source, which, first, count in spans:
            for target, (rows, parts) in enumerate(plans):
                for who, start, size, column, columns, down, along in parts:
                    low, high = max(first, start), min(first + count, start + size)
                    if low < high:
                        copies.append(
                            (index, source + low - first, high - low, column, columns)
                            + (target, which, who, rows, down + low - start, along)
                        )
    outs = [
        jax.ShapeDtypeStruct(
            (2 * chips * rows, max(p[6] + p[4] for p in parts)), held[0][0].dtype
        )
        for rows, parts in plans
    ]
    n_in = len(held)

    def kernel(place, *refs):
        sources, targets, sems = refs[:n_in], refs[n_in:-1], refs[-1]
        moves = []
        for i, c in enumerate(copies):
            index, row, count, column, columns, target, which, who, rows, down, along = c
            shard = 2 * (place[0] ^ which) + (place[1] ^ who)
            moves.append(
                pltpu.make_async_copy(
                    sources[index].at[pl.ds(row, count), pl.ds(column, columns)],
                    targets[target].at[
                        pl.ds(pl.multiple_of(shard * rows + down, 8), count),
                        pl.ds(along, columns),
                    ],
                    sems.at[i],
                )
            )
        for move in moves:
            move.start()
        for move in moves:
            move.wait()

    return pl.pallas_call(
        kernel,
        in_specs=[pl.BlockSpec(memory_space=pltpu.SMEM)]
        + [pl.BlockSpec(memory_space=pl.ANY)] * n_in,
        out_specs=[pl.BlockSpec(memory_space=pltpu.VMEM)] * len(outs),
        out_shape=outs,
        scratch_shapes=[pltpu.SemaphoreType.DMA((len(copies),))],
    )(place, *[x for x, _ in held])


def gradient_chunks(lefts, right, chips, place, tile, extra=0, into=None, first=0, shift=0, size=None, total=None):
    tokens, wide = lefts[0].shape[0], sum(x.shape[1] for x in lefts)
    size = size or right.shape[1]
    n = wide // chips
    shard = n // 2
    total = into[0].shape[1] if into else (total or size)
    given = list(into) if into else []

    def kernel(place, *refs):
        left_refs, right_ref = refs[: len(lefts)], refs[len(lefts)]
        outs = refs[len(lefts) + 1 + len(given) : -2]
        left_ref, pack_ref = refs[-2:]

        @pl.when(pl.program_id(0) == 0)
        def _():
            for i, ref in enumerate(left_refs):
                x = ref[...]
                if i:
                    x = jnp.concatenate([x[tokens // 2 :], x[: tokens // 2]], axis=0)
                hi, lo = halves(x.T)
                count = chips // len(left_refs)
                for c in range(count):
                    which = c if len(left_refs) == 1 else c + count * (place[1] ^ i)
                    at = pl.ds(pl.multiple_of((place[0] ^ which) * n, 16), n)
                    part = slice(c * n, (c + 1) * n)
                    left_ref[at, :tokens] = lo[part]
                    left_ref[at, tokens : 2 * tokens] = hi[part]
                    left_ref[at, 2 * tokens :] = hi[part]

        hi, lo = halves(right_ref[...])
        pack_ref[:tokens, :] = hi
        pack_ref[tokens : 2 * tokens, :] = lo
        pack_ref[2 * tokens :, :] = hi
        product = jnp.dot(left_ref[...], pack_ref[...], preferred_element_type=jnp.float32)
        for j in range(chips):
            for i in range(2):
                outs[j][i * (shard + extra) : i * (shard + extra) + shard, :] = product[
                    j * n + i * shard : j * n + (i + 1) * shard
                ]

    steps = size // tile
    return pl.pallas_call(
        kernel,
        grid_spec=pltpu.PrefetchScalarGridSpec(
            num_scalar_prefetch=1,
            grid=(steps,),
            in_specs=[pl.BlockSpec(x.shape, lambda i, place: (0, 0)) for x in lefts]
            + [pl.BlockSpec((tokens, tile), lambda i, place: (0, i + place[1] * (shift // tile)))]
            + [pl.BlockSpec(memory_space=pl.ANY) for _ in given],
            out_specs=[
                pl.BlockSpec((n + 2 * extra, tile), lambda i, place: (0, i + first // tile))
            ]
            * chips,
            scratch_shapes=[
                pltpu.VMEM((wide, 3 * tokens), jnp.bfloat16),
                pltpu.VMEM((3 * tokens, tile), jnp.bfloat16),
            ],
        ),
        out_shape=[jax.ShapeDtypeStruct((n + 2 * extra, total), jnp.float32)] * chips,
        input_output_aliases={2 + len(lefts) + i: i for i in range(len(given))},
    )(place, *lefts, right, *given)


def put_rows(chunks, table, place, shard, extra):
    count = len(chunks)

    def kernel(place, table_ref, *refs):
        outs, sems = refs[count:-1], refs[-1]
        moves = [
            pltpu.make_async_copy(
                table_ref.at[
                    pl.ds(pl.multiple_of((2 * (place[0] ^ j) + i) * extra, 8), extra), :
                ],
                outs[j].at[pl.ds(i * (shard + extra) + shard, extra), :],
                sems.at[2 * j + i],
            )
            for j in range(count)
            for i in range(2)
        ]
        for move in moves:
            move.start()
        for move in moves:
            move.wait()

    return pl.pallas_call(
        kernel,
        in_specs=[pl.BlockSpec(memory_space=pltpu.SMEM), pl.BlockSpec(memory_space=pltpu.VMEM)]
        + [pl.BlockSpec(memory_space=pl.ANY)] * count,
        out_specs=[pl.BlockSpec(memory_space=pl.ANY)] * count,
        out_shape=[jax.ShapeDtypeStruct(x.shape, x.dtype) for x in chunks],
        scratch_shapes=[pltpu.SemaphoreType.DMA((2 * count,))],
        input_output_aliases={2 + j: j for j in range(count)},
        name="put_rows",
    )(place, table, *chunks)


def scatter_chunks(chunks):
    n = chunks[0].shape[0]
    if len(chunks) == 4:
        half = n // 2
        via_x = flip(chunks[3][:half], 2)
        via_y = flip(chunks[3][half:], 4)
        to_y = flip(jnp.concatenate([chunks[2][:half] + via_x, chunks[2][half:]]), 4)
        to_x = flip(jnp.concatenate([chunks[1][:half], chunks[1][half:] + via_y]), 2)
        return [chunks[0], to_y, to_x]
    held = list(chunks)
    step = len(held) // 2
    while step:
        other = flip(jnp.concatenate(held[step:], axis=0), 2 * step)
        held = [held[i] + other[i * n : (i + 1) * n] for i in range(step)]
        step //= 2
    return held


def halo_moves(shards, reps):
    own_prev, other_prev, own_next, other_next = [], [], [], []
    for s in range(shards):
        for r in range(reps):
            here = s * reps + r
            if r > 0:
                own_prev.append((here - 1, here))
                other_prev.append((here - 1, here))
            else:
                source = s if s % 2 else s - 2
                if source >= 0:
                    own_prev.append((source * reps + reps - 1, here))
                source = s - 2 if s % 2 else s
                if source >= 0:
                    other_prev.append((source * reps + reps - 1, here))
            if r < reps - 1:
                own_next.append((here + 1, here))
                other_next.append((here + 1, here))
            else:
                source = s + 2 if s % 2 else s
                if source < shards:
                    own_next.append((source * reps, here))
                source = s if s % 2 else s + 2
                if source < shards:
                    other_next.append((source * reps, here))
    return own_prev, other_prev, own_next, other_next


def ordered(mine, theirs, odd, axis):
    size = mine.shape[axis]
    shape = list(mine.shape)
    shape[axis] = 2 * size
    both = jnp.zeros(tuple(shape), mine.dtype)
    both = lax.dynamic_update_slice_in_dim(both, mine, odd * size, axis)
    return lax.dynamic_update_slice_in_dim(both, theirs, (1 - odd) * size, axis)


def swap_halves(x):
    n = x.shape[0] // 2
    return jnp.concatenate([x[n:], x[:n]], axis=0)


def pair_sum(x):
    return x + swap_halves(partner(x))


def pick(x, index, size, axis):
    return lax.dynamic_slice_in_dim(x, index * size, size, axis)


def per_device(
    inputs,
    image_ids,
    output_gradient,
    first_norm_scale,
    first_norm_bias,
    w_qkv,
    bias_query,
    bias_value,
    w_output,
    bias_output,
    second_norm_scale,
    second_norm_bias,
    w_up,
    bias_up,
    w_down,
    bias_down,
):
    shards, reps = lax.axis_size("shard"), lax.axis_size("rep")
    chips = shards // 2
    shard, rep = lax.axis_index("shard"), lax.axis_index("rep")
    chip, odd = shard // 2, shard % 2
    axes = ("shard", "rep")
    own, width = inputs.shape
    rows = w_qkv.shape[0]
    mine = width // 2
    hidden = w_up.shape[1] // 2
    ext = own + 2 * REACH

    ids = (image_ids + 1).astype(jnp.float32)

    def with_ids(x, x_ids):
        line = jnp.pad(x_ids[None], ((0, PAD - 1), (0, width - x_ids.shape[0])))
        return jnp.concatenate([x, line], axis=0)

    forward = [(i, i + 1) for i in range(shards * reps - 1)]
    backward = [(b, a) for a, b in forward]
    low = lax.ppermute(with_ids(inputs[own - REACH :], ids[own - REACH :]), axes, forward)
    high = lax.ppermute(with_ids(inputs[:REACH], ids[:REACH]), axes, backward)
    g_two = jnp.concatenate([output_gradient, partner(output_gradient)], axis=0)

    small = jnp.concatenate(
        [
            first_norm_scale,
            first_norm_bias,
            second_norm_scale,
            second_norm_bias,
            bias_output,
            bias_down,
            bias_query,
            bias_value,
            bias_up,
        ]
    )
    lead = 3 * mine
    place = jnp.stack([chip, odd])
    small = jnp.pad(small, (0, -small.shape[0] % lead)).reshape(-1, lead)
    small = jnp.pad(small, ((0, -small.shape[0] % PAD), (0, 0)))
    extra = small.shape[0]

    def qkv_half(which):
        parts = [pick(w_qkv, 2 * i + which, mine, 1) for i in range(3)]
        return jnp.concatenate([jnp.concatenate(parts, axis=1), small])

    def rest_half(which):
        return [pick(w_up, which, hidden, 1), pick(w_down.T, which, hidden, 1)]

    first = partner(qkv_half(1 - odd))
    first = jnp.concatenate([qkv_half(odd), first])
    theirs = partner(jnp.concatenate(rest_half(1 - odd), axis=1))
    up_half, down_half = rest_half(odd)
    out_pair = jnp.concatenate([w_output[:, :mine], w_output[:, mine:]])
    second = jnp.concatenate(
        [jnp.concatenate([up_half, theirs[:, :hidden]]), out_pair], axis=1
    )
    third = jnp.concatenate([down_half, theirs[:, hidden:]])
    first_held, _ = gathered_pieces(first, chips)

    low, high, _ = lax.optimization_barrier((low, high, first_held[1][0]))
    ids_ext = jnp.concatenate([ids, low[REACH, :REACH], high[REACH, :REACH]])
    x_ext = jnp.concatenate([inputs, low[:REACH], high[:REACH]], axis=0)
    other_ext = partner(with_ids(x_ext, ids_ext))
    ids_two = jnp.stack([ids_ext, other_ext[ext, :ext]])
    ids_col, ids_row = ids_two[:, :own, None], ids_two[:, None, :]
    tokens = jnp.concatenate([x_ext, other_ext[:ext]], axis=0)

    second_held, sent = gathered_pieces(second, chips)
    third_held, sent = gathered_pieces(third, chips, sent)
    per = rows + extra
    wqkv, gathered_small = assemble(
        first_held,
        chips,
        place,
        [
            (rows, [(i, i * per, rows, 0, lead, 0, 0) for i in range(2)]),
            (extra, [(i, i * per + rows, extra, 0, lead, 0, 0) for i in range(2)]),
        ],
    )
    wup, out_own = assemble(
        second_held,
        chips,
        place,
        [
            (rows, [(i, i * rows, rows, 0, hidden, 0, 0) for i in range(2)]),
            (rows, [(0, i * rows, rows, hidden, mine, 0, i * mine) for i in range(2)]),
        ],
    )
    (wdown_t,) = assemble(
        third_held, chips, place, [(rows, [(i, i * rows, rows, 0, hidden, 0, 0) for i in range(2)])]
    )
    by_shard = out_own.reshape(2, chips // 2, 2, rows, width)

    def out_rows_of(half, parity):
        return pick(pick(by_shard, half, 1, 0), parity, 1, 2).reshape(chips // 2, rows, width)

    out_theirs = partner(out_rows_of(1 - odd, odd))
    out_ours = out_rows_of(odd, odd)
    wout = ordered(out_ours, out_theirs, odd, 1).reshape(mine, width)

    table = gathered_small.reshape(shards, extra * lead)

    def vector(start, size):
        return table[:, start : start + size].reshape(shards * size)

    first_scale, first_bias, second_scale, second_bias, bout, bdown, bq, bv = (
        vector(i * rows, rows) for i in range(8)
    )
    bup = pick(vector(8 * rows, bias_up.shape[0]), odd, hidden, 0)
    shift = jnp.concatenate(
        [pick(bq, odd, mine, 0), jnp.zeros((mine,), jnp.float32), pick(bv, odd, mine, 0)]
    )

    first_normalized, first_standardized, first_inverse_deviation = layer_norm_forward(
        tokens, first_scale, first_bias
    )
    proj = (matmul(first_normalized, wqkv) + shift).reshape(2, ext, lead)
    attended, lse = attention_forward(proj, ids_col, ids_row, own, mine)
    out_rows = attended.reshape(2 * own, mine)
    x_two = jnp.concatenate([tokens[:own], tokens[ext : ext + own]], axis=0)
    middle_state = x_two + pair_sum(matmul(out_rows, wout)) + bout

    second_normalized, second_standardized, second_inverse_deviation = layer_norm_forward(
        middle_state, second_scale, second_bias
    )
    pre = matmul(second_normalized, wup) + bup
    act, slope = gelu_parts(pre)
    down = matmul(act, wdown_t, ((1,), (1,)))
    outputs = middle_state[:own] + (down[:own] + partner(down[own:])) + bdown
    down_chunks = gradient_chunks([g_two], act, chips, place, hidden // 3)
    d_pre = matmul(g_two, wdown_t) * slope
    grad_bias_up = jnp.sum(d_pre, axis=0)
    middle_into = gradient_chunks(
        [second_normalized], d_pre, chips, place, mine, total=hidden + mine
    )
    d_second = pair_sum(matmul(d_pre, wup, ((1,), (1,))))
    gradient_middle = g_two + layer_norm_backward(
        d_second, second_standardized, second_inverse_deviation, second_scale
    )

    d_attended = matmul(gradient_middle, wout, ((1,), (1,)))
    other_rows = partner(out_rows)
    middle_chunks = gradient_chunks(
        [out_rows, other_rows],
        gradient_middle,
        chips,
        place,
        mine,
        into=middle_into,
        first=hidden,
        shift=mine,
        size=mine,
    )
    heads = mine // HEAD
    lse_rows = jnp.swapaxes(lse.reshape(2, own, heads, HEAD)[..., 0], 1, 2)
    member = (
        jnp.arange(mine)[None, :] // HEAD == jnp.arange(heads)[:, None]
    ).astype(jnp.float32)
    delta_rows = lax.dot_general(
        member,
        d_attended * out_rows,
        (((1,), (1,)), ((), ())),
        precision=EXACT,
        preferred_element_type=jnp.float32,
    )
    delta_rows = jnp.swapaxes(delta_rows.reshape(heads, 2, own), 0, 1)
    grads = d_attended.reshape(2, own, mine)
    stats = jnp.concatenate([lse_rows, delta_rows], axis=1)
    lines = -2 * heads % PAD + 2 * heads

    def edge(start):
        s = jnp.pad(
            stats[:, :, start : start + REACH],
            ((0, 0), (0, lines - 2 * heads), (0, mine - REACH)),
        )
        return jnp.concatenate([grads[:, start : start + REACH], s], axis=1)

    own_prev, other_prev, own_next, other_next = halo_moves(shards, reps)
    tail, head = edge(own - REACH), edge(0)
    at_end = (rep == reps - 1).astype(jnp.int32)
    at_start = (rep == 0).astype(jnp.int32)

    def block(x, index):
        return lax.dynamic_index_in_dim(x, index, 0, keepdims=False)

    prev = [
        lax.ppermute(block(tail, at_end), axes, own_prev),
        lax.ppermute(block(tail, 1 - at_end), axes, other_prev),
    ]
    following = [
        lax.ppermute(block(head, at_start), axes, own_next),
        lax.ppermute(block(head, 1 - at_start), axes, other_next),
    ]
    d_query = attention_queries(proj, grads, attended, lse, ids_col, ids_row, own, mine)
    grads_ext = jnp.stack(
        [
            jnp.concatenate([grads[b], prev[b][:REACH], following[b][:REACH]], axis=0)
            for b in range(2)
        ]
    )
    stats_ext = jnp.stack(
        [
            jnp.concatenate(
                [
                    stats[b],
                    prev[b][REACH : REACH + 2 * heads, :REACH],
                    following[b][REACH : REACH + 2 * heads, :REACH],
                ],
                axis=1,
            )
            for b in range(2)
        ]
    )
    d_key, d_value = attention_keys(
        proj, grads_ext, stats_ext[:, :heads], stats_ext[:, heads:], ids_col, ids_row, own, mine
    )
    d_proj = jnp.concatenate([d_query, d_key, d_value], axis=2).reshape(2 * own, lead)
    normalized_two = jnp.concatenate(
        [first_normalized[:own], first_normalized[ext : ext + own]], axis=0
    )
    last_chunks = gradient_chunks([normalized_two], d_proj, chips, place, mine, extra=PAD)
    d_first = matmul(d_proj, wqkv, ((1,), (1,)))
    d_first = d_first[:own] + partner(d_first[own:])
    gradient_of_input = gradient_middle[:own] + layer_norm_backward(
        d_first, first_standardized[:own], first_inverse_deviation[:own], first_scale
    )

    sums = jnp.sum(d_proj, axis=0)

    def spread(half):
        full = jnp.zeros((2 * half.shape[0],), jnp.float32)
        return lax.dynamic_update_slice_in_dim(full, half, odd * half.shape[0], 0)

    small_sums = [
        jnp.sum(d_first * first_standardized[:own], axis=0),
        jnp.sum(d_first, axis=0),
        jnp.sum(d_second[:own] * second_standardized[:own], axis=0),
        jnp.sum(d_second[:own], axis=0),
        jnp.sum(gradient_middle[:own], axis=0),
        jnp.sum(output_gradient, axis=0),
        spread(sums[:mine]),
        spread(sums[2 * mine :]),
        spread(grad_bias_up),
    ]
    table = jnp.concatenate([v.reshape(shards, -1) for v in small_sums], axis=1)
    lines = -(-table.shape[1] // lead)
    table = jnp.pad(table, ((0, 0), (0, lines * lead - table.shape[1])))
    table = jnp.pad(table.reshape(shards, lines, lead), ((0, 0), (0, PAD - lines), (0, 0)))
    last_chunks = put_rows(last_chunks, table.reshape(shards * PAD, lead), place, rows, PAD)

    def finish(parts):
        n = parts[0].shape[0] // 2

        def rows_of(which):
            picked = [pick(x, which, n, 0) for x in parts]
            return sum(picked[1:], picked[0])

        theirs = partner(rows_of(1 - odd))
        return rows_of(odd), theirs

    down_mine, down_theirs = finish(scatter_chunks(down_chunks))
    middle_mine, middle_theirs = finish(scatter_chunks(middle_chunks))
    last_mine, last_theirs = finish(scatter_chunks(last_chunks))
    small_mine, small_theirs = last_mine[rows:], last_theirs[rows:]
    last_mine, last_theirs = last_mine[:rows], last_theirs[:rows]

    total_down = lax.psum(ordered(down_mine, down_theirs, odd, 1), "rep")
    total_down_t = total_down.T
    grad_up_total = ordered(middle_mine[:, :hidden], middle_theirs[:, :hidden], odd, 1)
    grad_out_total = ordered(middle_mine[:, hidden:], middle_theirs[:, hidden:], odd, 1)
    grad_up_total, grad_out_total, total_down = lax.optimization_barrier(
        (grad_up_total, grad_out_total, total_down)
    )
    grad_up_total, grad_out_total = lax.psum((grad_up_total, grad_out_total), "rep")
    qkv_total = jnp.concatenate(
        [
            ordered(last_mine[:, i * mine : (i + 1) * mine], last_theirs[:, i * mine : (i + 1) * mine], odd, 1)
            for i in range(3)
        ],
        axis=1,
    )
    qkv_total = jnp.concatenate(
        [qkv_total, (small_mine + small_theirs).reshape(-1, 2 * lead)], axis=0
    )
    qkv_total, grad_up_total, grad_out_total = lax.optimization_barrier(
        (qkv_total, grad_up_total, grad_out_total)
    )
    qkv_total = lax.psum(qkv_total, "rep")
    qkv_total, small_total = qkv_total[:rows], qkv_total[rows:]
    small_total = small_total.reshape(-1)
    small_out = [small_total[i * rows : (i + 1) * rows] for i in range(8)]
    up_bias_out = small_total[8 * rows : 8 * rows + bias_up.shape[0]]
    return (
        outputs,
        gradient_of_input,
        small_out[0],
        small_out[1],
        qkv_total,
        small_out[6],
        small_out[7],
        grad_out_total,
        small_out[4],
        small_out[2],
        small_out[3],
        grad_up_total,
        up_bias_out,
        total_down_t,
        small_out[5],
    )


def solution(mesh):
    placed = (
        P(("shard", "rep"), None),
        P(("shard", "rep")),
        P(("shard", "rep"), None),
        P("shard"),
        P("shard"),
        P("shard", None),
        P("shard"),
        P("shard"),
        P("shard", None),
        P("shard"),
        P("shard"),
        P("shard"),
        P("shard", None),
        P("shard"),
        P(None, "shard"),
        P("shard"),
    )

    return jax.shard_map(
        per_device,
        mesh=mesh,
        in_specs=placed,
        out_specs=(
            P(("shard", "rep"), None),
            P(("shard", "rep"), None),
            P("shard"),
            P("shard"),
            P("shard", None),
            P("shard"),
            P("shard"),
            P("shard", None),
            P("shard"),
            P("shard"),
            P("shard"),
            P("shard", None),
            P("shard"),
            P(None, "shard"),
            P("shard"),
        ),
        check_vma=False,
    )
```

```python
import math

import jax
import jax.numpy as jnp
from jax import lax
from jax.experimental import pallas as pl
from jax.experimental.pallas import tpu as pltpu
from jax.sharding import PartitionSpec as P


HEAD = 64
REACH = 200
PAD = 8
HIGH = lax.Precision.HIGH
EXACT = lax.Precision.HIGHEST


SHARD, REP = "shard", "rep"


def matmul(left, right, dims=((1,), (0,))):
    return lax.dot_general(
        left, right, (dims, ((), ())), precision=HIGH, preferred_element_type=jnp.float32
    )


def layer_norm_forward(rows, norm_scale, norm_bias):
    centered_input = rows - jnp.mean(rows, axis=-1, keepdims=True)
    inverse_deviation = lax.rsqrt(
        jnp.mean(centered_input * centered_input, axis=-1, keepdims=True) + 1e-06
    )
    standardized = centered_input * inverse_deviation
    return (standardized * norm_scale + norm_bias, standardized, inverse_deviation)


def layer_norm_backward(upstream_gradient, standardized, inverse_deviation, norm_scale):
    scaled_values = upstream_gradient * norm_scale
    return inverse_deviation * (
        scaled_values
        - jnp.mean(scaled_values, axis=-1, keepdims=True)
        - standardized * jnp.mean(scaled_values * standardized, axis=-1, keepdims=True)
    )


def gelu_parts(pre):
    cdf = 0.5 * (1.0 + jax.scipy.special.erf(pre / math.sqrt(2.0)))
    slope = cdf + pre * jnp.exp(-0.5 * pre * pre) / math.sqrt(2.0 * math.pi)
    return (pre * cdf, slope)


def halves(x):
    hi = x.astype(jnp.bfloat16)
    lo = (x - hi.astype(jnp.float32)).astype(jnp.bfloat16)
    return hi, lo


def left3(x):
    hi, lo = halves(x)
    return jnp.concatenate([hi, hi, lo], axis=1)


def right3(x):
    hi, lo = halves(x)
    return jnp.concatenate([hi, lo, hi], axis=1)


def dot_nt(a, b):
    return lax.dot_general(a, b, (((1,), (1,)), ((), ())), preferred_element_type=jnp.float32)


def weighted(p, x):
    hi, lo = halves(p)
    xh, xl = halves(x)
    both = jnp.dot(hi, jnp.concatenate([xh, xl], axis=1), preferred_element_type=jnp.float32)
    return both[:, :HEAD] + both[:, HEAD:] + jnp.dot(lo, xh, preferred_element_type=jnp.float32)


def forward_kernel(q_ref, k_ref, v_ref, idc_ref, idr_ref, out_ref, lse_ref):
    same = idc_ref[0] == idr_ref[0]
    outs, lses = [], []
    for h in range(2):
        cols = slice(h * HEAD, (h + 1) * HEAD)
        q = q_ref[0][:, cols] * (1.0 / math.sqrt(HEAD))
        s = dot_nt(left3(q), right3(k_ref[0][:, cols]))
        s = jnp.where(same, s, -1e30)
        top = jnp.max(s, axis=1, keepdims=True)
        w = jnp.exp(s - top)
        total = jnp.sum(w, axis=1, keepdims=True)
        outs.append(weighted(w, v_ref[0][:, cols]) / total)
        lses.append(jnp.broadcast_to(top + jnp.log(total), (q.shape[0], HEAD)))
    out_ref[0] = jnp.concatenate(outs, axis=1)
    lse_ref[0] = jnp.concatenate(lses, axis=1)


def query_kernel(q_ref, k_ref, v_ref, g_ref, out_ref, lse_ref, idc_ref, idr_ref, dq_ref):
    same = idc_ref[0] == idr_ref[0]
    scale = 1.0 / math.sqrt(HEAD)
    outs = []
    for h in range(2):
        cols = slice(h * HEAD, (h + 1) * HEAD)
        q, k = q_ref[0][:, cols] * scale, k_ref[0][:, cols]
        g = g_ref[0][:, cols]
        lse = lse_ref[0][:, h * HEAD : h * HEAD + 1]
        delta = jnp.sum(g * out_ref[0][:, cols], axis=1, keepdims=True)
        s = dot_nt(left3(q), right3(k))
        p = jnp.exp(jnp.where(same, s - lse, -1e30))
        d_p = dot_nt(left3(g), right3(v_ref[0][:, cols]))
        outs.append(weighted(p * (d_p - delta), k) * scale)
    dq_ref[0] = jnp.concatenate(outs, axis=1)


def key_kernel(q_ref, g_ref, lse_ref, delta_ref, k_ref, v_ref, idc_ref, idr_ref, dk_ref, dv_ref):
    same = idc_ref[0] == idr_ref[0]
    scale = 1.0 / math.sqrt(HEAD)
    d_k, d_v = [], []
    for h in range(2):
        cols = slice(h * HEAD, (h + 1) * HEAD)
        q = q_ref[0][:, cols] * scale
        g = g_ref[0][:, cols]
        row = 2 * pl.program_id(1) + h
        lse = lse_ref[0, pl.ds(row, 1), :]
        delta = delta_ref[0, pl.ds(row, 1), :]
        s = dot_nt(left3(k_ref[0][:, cols]), right3(q))
        p = jnp.exp(jnp.where(same, s - lse, -1e30))
        d_p = dot_nt(left3(v_ref[0][:, cols]), right3(g))
        d_v.append(weighted(p, g))
        d_k.append(weighted(p * (d_p - delta), q))
    dk_ref[0] = jnp.concatenate(d_k, axis=1)
    dv_ref[0] = jnp.concatenate(d_v, axis=1)


def head_block(rows, first=0):
    return pl.BlockSpec((1, rows, 2 * HEAD), lambda b, h: (b, 0, first + h))


def whole_block(*shape):
    return pl.BlockSpec((1,) + shape, lambda b, h: (b, 0, 0))


def attention_forward(proj, ids_col, ids_row, own, width):
    blocks, ext, _ = proj.shape
    pairs = width // (2 * HEAD)
    return pl.pallas_call(
        forward_kernel,
        grid=(blocks, pairs),
        in_specs=[
            head_block(own),
            head_block(ext, pairs),
            head_block(ext, 2 * pairs),
            whole_block(own, 1),
            whole_block(1, ext),
        ],
        out_specs=[head_block(own), head_block(own)],
        out_shape=[jax.ShapeDtypeStruct((blocks, own, width), jnp.float32)] * 2,
        name="af",
    )(proj, proj, proj, ids_col, ids_row)


def attention_queries(proj, grads, out, lse, ids_col, ids_row, own, width):
    blocks, ext, _ = proj.shape
    pairs = width // (2 * HEAD)
    return pl.pallas_call(
        query_kernel,
        grid=(blocks, pairs),
        in_specs=[
            head_block(own),
            head_block(ext, pairs),
            head_block(ext, 2 * pairs),
            head_block(own),
            head_block(own),
            head_block(own),
            whole_block(own, 1),
            whole_block(1, ext),
        ],
        out_specs=head_block(own),
        out_shape=jax.ShapeDtypeStruct((blocks, own, width), jnp.float32),
        name="aq",
    )(proj, proj, proj, grads, out, lse, ids_col, ids_row)


def attention_keys(proj, grads, lse_rows, delta_rows, ids_col, ids_row, own, width):
    blocks, ext, _ = proj.shape
    pairs = width // (2 * HEAD)
    rows = lse_rows.shape[1]
    return pl.pallas_call(
        key_kernel,
        grid=(blocks, pairs),
        in_specs=[
            head_block(ext),
            head_block(ext),
            whole_block(rows, ext),
            whole_block(rows, ext),
            head_block(own, pairs),
            head_block(own, 2 * pairs),
            whole_block(own, 1),
            whole_block(1, ext),
        ],
        out_specs=[head_block(own), head_block(own)],
        out_shape=[jax.ShapeDtypeStruct((blocks, own, width), jnp.float32)] * 2,
        name="ak",
    )(proj, grads, lse_rows, delta_rows, proj, proj, ids_col, ids_row)


def flip(x, bit):
    count = lax.axis_size(SHARD)
    return lax.ppermute(x, SHARD, [(i, i ^ bit) for i in range(count)])


def partner(x):
    return flip(x, 1)


def gathered_pieces(piece, chips, after=None):
    rows = piece.shape[0]
    if after is not None:
        piece, after = lax.optimization_barrier((piece, after))
    if chips == 4:
        half = rows // 2
        from_x, from_y = flip(piece, 2), flip(piece, 4)
        upper, lower = flip(from_x[:half], 4), flip(from_y[half:], 2)
        held = [
            (piece, [(0, 0, 0, rows)]),
            (from_x, [(0, 1, 0, rows)]),
            (from_y, [(0, 2, 0, rows)]),
            (upper, [(0, 3, 0, half)]),
            (lower, [(0, 3, half, half)]),
        ]
        return held, (upper, lower)
    held = [(piece, [(0, 0, 0, rows)])]
    step = 1
    while step < chips:
        joined = jnp.concatenate([x for x, _ in held], axis=0)
        spans = [(i * rows, step + i, 0, rows) for i in range(step)]
        held.append((flip(joined, 2 * step), spans))
        step *= 2
    return held, held[-1][0]


def assemble(held, chips, place, plans):
    copies = []
    for index, (_, spans) in enumerate(held):
        for source, which, first, count in spans:
            for target, (rows, parts) in enumerate(plans):
                for who, start, size, column, columns, down, along in parts:
                    low, high = max(first, start), min(first + count, start + size)
                    if low < high:
                        copies.append(
                            (index, source + low - first, high - low, column, columns)
                            + (target, which, who, rows, down + low - start, along)
                        )
    outs = [
        jax.ShapeDtypeStruct(
            (2 * chips * rows, max(p[6] + p[4] for p in parts)), held[0][0].dtype
        )
        for rows, parts in plans
    ]
    n_in = len(held)

    def kernel(place, *refs):
        sources, targets, sems = refs[:n_in], refs[n_in:-1], refs[-1]
        moves = []
        for i, c in enumerate(copies):
            index, row, count, column, columns, target, which, who, rows, down, along = c
            shard = 2 * (place[0] ^ which) + (place[1] ^ who)
            moves.append(
                pltpu.make_async_copy(
                    sources[index].at[pl.ds(row, count), pl.ds(column, columns)],
                    targets[target].at[
                        pl.ds(pl.multiple_of(shard * rows + down, 8), count),
                        pl.ds(along, columns),
                    ],
                    sems.at[i],
                )
            )
        for move in moves:
            move.start()
        for move in moves:
            move.wait()

    return pl.pallas_call(
        kernel,
        in_specs=[pl.BlockSpec(memory_space=pltpu.SMEM)]
        + [pl.BlockSpec(memory_space=pl.ANY)] * n_in,
        out_specs=[pl.BlockSpec(memory_space=pltpu.VMEM)] * len(outs),
        out_shape=outs,
        scratch_shapes=[pltpu.SemaphoreType.DMA((len(copies),))],
    )(place, *[x for x, _ in held])


def gradient_chunks(lefts, right, chips, place, tile, extra=0, into=None, first=0, shift=0, size=None, total=None):
    tokens, wide = lefts[0].shape[0], sum(x.shape[1] for x in lefts)
    size = size or right.shape[1]
    n = wide // chips
    shard = n // 2
    total = into[0].shape[1] if into else (total or size)
    given = list(into) if into else []

    def kernel(place, *refs):
        left_refs, right_ref = refs[: len(lefts)], refs[len(lefts)]
        outs = refs[len(lefts) + 1 + len(given) : -2]
        left_ref, pack_ref = refs[-2:]

        @pl.when(pl.program_id(0) == 0)
        def _():
            for i, ref in enumerate(left_refs):
                x = ref[...]
                if i:
                    x = jnp.concatenate([x[tokens // 2 :], x[: tokens // 2]], axis=0)
                hi, lo = halves(x.T)
                count = chips // len(left_refs)
                for c in range(count):
                    which = c if len(left_refs) == 1 else c + count * (place[1] ^ i)
                    at = pl.ds(pl.multiple_of((place[0] ^ which) * n, 16), n)
                    part = slice(c * n, (c + 1) * n)
                    left_ref[at, :tokens] = lo[part]
                    left_ref[at, tokens : 2 * tokens] = hi[part]
                    left_ref[at, 2 * tokens :] = hi[part]

        hi, lo = halves(right_ref[...])
        pack_ref[:tokens, :] = hi
        pack_ref[tokens : 2 * tokens, :] = lo
        pack_ref[2 * tokens :, :] = hi
        product = jnp.dot(left_ref[...], pack_ref[...], preferred_element_type=jnp.float32)
        for j in range(chips):
            for i in range(2):
                outs[j][i * (shard + extra) : i * (shard + extra) + shard, :] = product[
                    j * n + i * shard : j * n + (i + 1) * shard
                ]

    steps = size // tile
    return pl.pallas_call(
        kernel,
        grid_spec=pltpu.PrefetchScalarGridSpec(
            num_scalar_prefetch=1,
            grid=(steps,),
            in_specs=[pl.BlockSpec(x.shape, lambda i, place: (0, 0)) for x in lefts]
            + [pl.BlockSpec((tokens, tile), lambda i, place: (0, i + place[1] * (shift // tile)))]
            + [pl.BlockSpec(memory_space=pl.ANY) for _ in given],
            out_specs=[
                pl.BlockSpec((n + 2 * extra, tile), lambda i, place: (0, i + first // tile))
            ]
            * chips,
            scratch_shapes=[
                pltpu.VMEM((wide, 3 * tokens), jnp.bfloat16),
                pltpu.VMEM((3 * tokens, tile), jnp.bfloat16),
            ],
        ),
        out_shape=[jax.ShapeDtypeStruct((n + 2 * extra, total), jnp.float32)] * chips,
        input_output_aliases={2 + len(lefts) + i: i for i in range(len(given))},
    )(place, *lefts, right, *given)


def put_rows(chunks, table, place, shard, extra):
    count = len(chunks)

    def kernel(place, table_ref, *refs):
        outs, sems = refs[count:-1], refs[-1]
        moves = [
            pltpu.make_async_copy(
                table_ref.at[
                    pl.ds(pl.multiple_of((2 * (place[0] ^ j) + i) * extra, 8), extra), :
                ],
                outs[j].at[pl.ds(i * (shard + extra) + shard, extra), :],
                sems.at[2 * j + i],
            )
            for j in range(count)
            for i in range(2)
        ]
        for move in moves:
            move.start()
        for move in moves:
            move.wait()

    return pl.pallas_call(
        kernel,
        in_specs=[pl.BlockSpec(memory_space=pltpu.SMEM), pl.BlockSpec(memory_space=pltpu.VMEM)]
        + [pl.BlockSpec(memory_space=pl.ANY)] * count,
        out_specs=[pl.BlockSpec(memory_space=pl.ANY)] * count,
        out_shape=[jax.ShapeDtypeStruct(x.shape, x.dtype) for x in chunks],
        scratch_shapes=[pltpu.SemaphoreType.DMA((2 * count,))],
        input_output_aliases={2 + j: j for j in range(count)},
        name="pr",
    )(place, table, *chunks)


def scatter_chunks(chunks):
    n = chunks[0].shape[0]
    if len(chunks) == 4:
        half = n // 2
        via_x = flip(chunks[3][:half], 2)
        via_y = flip(chunks[3][half:], 4)
        to_y = flip(jnp.concatenate([chunks[2][:half] + via_x, chunks[2][half:]]), 4)
        to_x = flip(jnp.concatenate([chunks[1][:half], chunks[1][half:] + via_y]), 2)
        return [chunks[0], to_y, to_x]
    held = list(chunks)
    step = len(held) // 2
    while step:
        other = flip(jnp.concatenate(held[step:], axis=0), 2 * step)
        held = [held[i] + other[i * n : (i + 1) * n] for i in range(step)]
        step //= 2
    return held


def halo_moves(shards, reps):
    own_prev, other_prev, own_next, other_next = [], [], [], []
    for s in range(shards):
        for r in range(reps):
            here = s * reps + r
            if r > 0:
                own_prev.append((here - 1, here))
                other_prev.append((here - 1, here))
            else:
                source = s if s % 2 else s - 2
                if source >= 0:
                    own_prev.append((source * reps + reps - 1, here))
                source = s - 2 if s % 2 else s
                if source >= 0:
                    other_prev.append((source * reps + reps - 1, here))
            if r < reps - 1:
                own_next.append((here + 1, here))
                other_next.append((here + 1, here))
            else:
                source = s + 2 if s % 2 else s
                if source < shards:
                    own_next.append((source * reps, here))
                source = s if s % 2 else s + 2
                if source < shards:
                    other_next.append((source * reps, here))
    return own_prev, other_prev, own_next, other_next


def ordered(mine, theirs, odd, axis):
    size = mine.shape[axis]
    shape = list(mine.shape)
    shape[axis] = 2 * size
    both = jnp.zeros(tuple(shape), mine.dtype)
    both = lax.dynamic_update_slice_in_dim(both, mine, odd * size, axis)
    return lax.dynamic_update_slice_in_dim(both, theirs, (1 - odd) * size, axis)


def swap_halves(x):
    n = x.shape[0] // 2
    return jnp.concatenate([x[n:], x[:n]], axis=0)


def pair_sum(x):
    return x + swap_halves(partner(x))


def pick(x, index, size, axis):
    return lax.dynamic_slice_in_dim(x, index * size, size, axis)


def per_device(
    inputs,
    image_ids,
    output_gradient,
    first_norm_scale,
    first_norm_bias,
    w_qkv,
    bias_query,
    bias_value,
    w_output,
    bias_output,
    second_norm_scale,
    second_norm_bias,
    w_up,
    bias_up,
    w_down,
    bias_down,
):
    shards, reps = lax.axis_size(SHARD), lax.axis_size(REP)
    chips = shards // 2
    shard, rep = lax.axis_index(SHARD), lax.axis_index(REP)
    chip, odd = shard // 2, shard % 2
    axes = (SHARD, REP)
    own, width = inputs.shape
    rows = w_qkv.shape[0]
    mine = width // 2
    hidden = w_up.shape[1] // 2
    ext = own + 2 * REACH

    ids = (image_ids + 1).astype(jnp.float32)

    def with_ids(x, x_ids):
        line = jnp.pad(x_ids[None], ((0, PAD - 1), (0, width - x_ids.shape[0])))
        return jnp.concatenate([x, line], axis=0)

    forward = [(i, i + 1) for i in range(shards * reps - 1)]
    backward = [(b, a) for a, b in forward]
    low = lax.ppermute(with_ids(inputs[own - REACH :], ids[own - REACH :]), axes, forward)
    high = lax.ppermute(with_ids(inputs[:REACH], ids[:REACH]), axes, backward)
    g_two = jnp.concatenate([output_gradient, partner(output_gradient)], axis=0)

    small = jnp.concatenate(
        [
            first_norm_scale,
            first_norm_bias,
            second_norm_scale,
            second_norm_bias,
            bias_output,
            bias_down,
            bias_query,
            bias_value,
            bias_up,
        ]
    )
    lead = 3 * mine
    place = jnp.stack([chip, odd])
    small = jnp.pad(small, (0, -small.shape[0] % lead)).reshape(-1, lead)
    small = jnp.pad(small, ((0, -small.shape[0] % PAD), (0, 0)))
    extra = small.shape[0]

    def qkv_half(which):
        parts = [pick(w_qkv, 2 * i + which, mine, 1) for i in range(3)]
        return jnp.concatenate([jnp.concatenate(parts, axis=1), small])

    def rest_half(which):
        return [pick(w_up, which, hidden, 1), pick(w_down.T, which, hidden, 1)]

    first = partner(qkv_half(1 - odd))
    first = jnp.concatenate([qkv_half(odd), first])
    theirs = partner(jnp.concatenate(rest_half(1 - odd), axis=1))
    up_half, down_half = rest_half(odd)
    out_pair = jnp.concatenate([w_output[:, :mine], w_output[:, mine:]])
    second = jnp.concatenate(
        [jnp.concatenate([up_half, theirs[:, :hidden]]), out_pair], axis=1
    )
    third = jnp.concatenate([down_half, theirs[:, hidden:]])
    first_held, _ = gathered_pieces(first, chips)

    low, high, _ = lax.optimization_barrier((low, high, first_held[1][0]))
    ids_ext = jnp.concatenate([ids, low[REACH, :REACH], high[REACH, :REACH]])
    x_ext = jnp.concatenate([inputs, low[:REACH], high[:REACH]], axis=0)
    other_ext = partner(with_ids(x_ext, ids_ext))
    ids_two = jnp.stack([ids_ext, other_ext[ext, :ext]])
    ids_col, ids_row = ids_two[:, :own, None], ids_two[:, None, :]
    tokens = jnp.concatenate([x_ext, other_ext[:ext]], axis=0)

    second_held, sent = gathered_pieces(second, chips)
    third_held, sent = gathered_pieces(third, chips, sent)
    per = rows + extra
    wqkv, gathered_small = assemble(
        first_held,
        chips,
        place,
        [
            (rows, [(i, i * per, rows, 0, lead, 0, 0) for i in range(2)]),
            (extra, [(i, i * per + rows, extra, 0, lead, 0, 0) for i in range(2)]),
        ],
    )
    wup, out_own = assemble(
        second_held,
        chips,
        place,
        [
            (rows, [(i, i * rows, rows, 0, hidden, 0, 0) for i in range(2)]),
            (rows, [(0, i * rows, rows, hidden, mine, 0, i * mine) for i in range(2)]),
        ],
    )
    (wdown_t,) = assemble(
        third_held, chips, place, [(rows, [(i, i * rows, rows, 0, hidden, 0, 0) for i in range(2)])]
    )
    by_shard = out_own.reshape(2, chips // 2, 2, rows, width)

    def out_rows_of(half, parity):
        return pick(pick(by_shard, half, 1, 0), parity, 1, 2).reshape(chips // 2, rows, width)

    out_theirs = partner(out_rows_of(1 - odd, odd))
    out_ours = out_rows_of(odd, odd)
    wout = ordered(out_ours, out_theirs, odd, 1).reshape(mine, width)

    table = gathered_small.reshape(shards, extra * lead)

    def vector(start, size):
        return table[:, start : start + size].reshape(shards * size)

    first_scale, first_bias, second_scale, second_bias, bout, bdown, bq, bv = (
        vector(i * rows, rows) for i in range(8)
    )
    bup = pick(vector(8 * rows, bias_up.shape[0]), odd, hidden, 0)
    shift = jnp.concatenate(
        [pick(bq, odd, mine, 0), jnp.zeros((mine,), jnp.float32), pick(bv, odd, mine, 0)]
    )

    first_normalized, first_standardized, first_inverse_deviation = layer_norm_forward(
        tokens, first_scale, first_bias
    )
    proj = matmul(first_normalized, wqkv) + shift
    proj = proj.reshape(2, ext, lead)
    attended, lse = attention_forward(proj, ids_col, ids_row, own, mine)
    out_rows = attended.reshape(2 * own, mine)
    x_two = jnp.concatenate([tokens[:own], tokens[ext : ext + own]], axis=0)
    middle_state = x_two + pair_sum(matmul(out_rows, wout)) + bout

    second_normalized, second_standardized, second_inverse_deviation = layer_norm_forward(
        middle_state, second_scale, second_bias
    )
    pre = matmul(second_normalized, wup) + bup
    act, slope = gelu_parts(pre)
    down = matmul(act, wdown_t, ((1,), (1,)))
    outputs = middle_state[:own] + (down[:own] + partner(down[own:])) + bdown
    down_chunks = gradient_chunks([g_two], act, chips, place, hidden // 3)
    d_pre = matmul(g_two, wdown_t) * slope
    grad_bias_up = jnp.sum(d_pre, axis=0)
    middle_into = gradient_chunks(
        [second_normalized], d_pre, chips, place, mine, total=hidden + mine
    )
    d_second = pair_sum(matmul(d_pre, wup, ((1,), (1,))))
    gradient_middle = g_two + layer_norm_backward(
        d_second, second_standardized, second_inverse_deviation, second_scale
    )

    d_attended = matmul(gradient_middle, wout, ((1,), (1,)))
    other_rows = partner(out_rows)
    middle_chunks = gradient_chunks(
        [out_rows, other_rows],
        gradient_middle,
        chips,
        place,
        mine,
        into=middle_into,
        first=hidden,
        shift=mine,
        size=mine,
    )
    heads = mine // HEAD
    lse_rows = jnp.swapaxes(lse.reshape(2, own, heads, HEAD)[..., 0], 1, 2)
    member = (
        jnp.arange(mine)[None, :] // HEAD == jnp.arange(heads)[:, None]
    ).astype(jnp.float32)
    delta_rows = lax.dot_general(
        member,
        d_attended * out_rows,
        (((1,), (1,)), ((), ())),
        precision=EXACT,
        preferred_element_type=jnp.float32,
    )
    delta_rows = jnp.swapaxes(delta_rows.reshape(heads, 2, own), 0, 1)
    grads = d_attended.reshape(2, own, mine)
    stats = jnp.concatenate([lse_rows, delta_rows], axis=1)
    lines = -2 * heads % PAD + 2 * heads

    def edge(start):
        s = jnp.pad(
            stats[:, :, start : start + REACH],
            ((0, 0), (0, lines - 2 * heads), (0, mine - REACH)),
        )
        return jnp.concatenate([grads[:, start : start + REACH], s], axis=1)

    own_prev, other_prev, own_next, other_next = halo_moves(shards, reps)
    tail, head = edge(own - REACH), edge(0)
    at_end = (rep == reps - 1).astype(jnp.int32)
    at_start = (rep == 0).astype(jnp.int32)

    def block(x, index):
        return lax.dynamic_index_in_dim(x, index, 0, keepdims=False)

    prev = [
        lax.ppermute(block(tail, at_end), axes, own_prev),
        lax.ppermute(block(tail, 1 - at_end), axes, other_prev),
    ]
    following = [
        lax.ppermute(block(head, at_start), axes, own_next),
        lax.ppermute(block(head, 1 - at_start), axes, other_next),
    ]
    d_query = attention_queries(proj, grads, attended, lse, ids_col, ids_row, own, mine)
    grads_ext = jnp.stack(
        [
            jnp.concatenate([grads[b], prev[b][:REACH], following[b][:REACH]], axis=0)
            for b in range(2)
        ]
    )
    stats_ext = jnp.stack(
        [
            jnp.concatenate(
                [
                    stats[b],
                    prev[b][REACH : REACH + 2 * heads, :REACH],
                    following[b][REACH : REACH + 2 * heads, :REACH],
                ],
                axis=1,
            )
            for b in range(2)
        ]
    )
    d_key, d_value = attention_keys(
        proj, grads_ext, stats_ext[:, :heads], stats_ext[:, heads:], ids_col, ids_row, own, mine
    )
    d_proj = jnp.concatenate([d_query, d_key, d_value], axis=2).reshape(2 * own, lead)
    normalized_two = jnp.concatenate(
        [first_normalized[:own], first_normalized[ext : ext + own]], axis=0
    )
    last_chunks = gradient_chunks([normalized_two], d_proj, chips, place, mine, extra=PAD)
    d_first = matmul(d_proj, wqkv, ((1,), (1,)))
    d_first = d_first[:own] + partner(d_first[own:])
    gradient_of_input = gradient_middle[:own] + layer_norm_backward(
        d_first, first_standardized[:own], first_inverse_deviation[:own], first_scale
    )

    sums = jnp.sum(d_proj, axis=0)

    def spread(half):
        full = jnp.zeros((2 * half.shape[0],), jnp.float32)
        return lax.dynamic_update_slice_in_dim(full, half, odd * half.shape[0], 0)

    small_sums = [
        jnp.sum(d_first * first_standardized[:own], axis=0),
        jnp.sum(d_first, axis=0),
        jnp.sum(d_second[:own] * second_standardized[:own], axis=0),
        jnp.sum(d_second[:own], axis=0),
        jnp.sum(gradient_middle[:own], axis=0),
        jnp.sum(output_gradient, axis=0),
        spread(sums[:mine]),
        spread(sums[2 * mine :]),
        spread(grad_bias_up),
    ]
    table = jnp.concatenate([v.reshape(shards, -1) for v in small_sums], axis=1)
    lines = -(-table.shape[1] // lead)
    table = jnp.pad(table, ((0, 0), (0, lines * lead - table.shape[1])))
    table = jnp.pad(table.reshape(shards, lines, lead), ((0, 0), (0, PAD - lines), (0, 0)))
    last_chunks = put_rows(last_chunks, table.reshape(shards * PAD, lead), place, rows, PAD)

    def finish(parts):
        n = parts[0].shape[0] // 2

        def rows_of(which):
            picked = [pick(x, which, n, 0) for x in parts]
            return sum(picked[1:], picked[0])

        theirs = partner(rows_of(1 - odd))
        return rows_of(odd), theirs

    down_mine, down_theirs = finish(scatter_chunks(down_chunks))
    middle_mine, middle_theirs = finish(scatter_chunks(middle_chunks))
    last_mine, last_theirs = finish(scatter_chunks(last_chunks))
    small_mine, small_theirs = last_mine[rows:], last_theirs[rows:]
    last_mine, last_theirs = last_mine[:rows], last_theirs[:rows]

    total_down = lax.psum(ordered(down_mine, down_theirs, odd, 1), REP)
    total_down_t = total_down.T
    grad_up_total = ordered(middle_mine[:, :hidden], middle_theirs[:, :hidden], odd, 1)
    grad_out_total = ordered(middle_mine[:, hidden:], middle_theirs[:, hidden:], odd, 1)
    grad_up_total, grad_out_total, total_down = lax.optimization_barrier(
        (grad_up_total, grad_out_total, total_down)
    )
    grad_up_total, grad_out_total = lax.psum((grad_up_total, grad_out_total), REP)
    qkv_total = jnp.concatenate(
        [
            ordered(last_mine[:, i * mine : (i + 1) * mine], last_theirs[:, i * mine : (i + 1) * mine], odd, 1)
            for i in range(3)
        ],
        axis=1,
    )
    qkv_total = jnp.concatenate(
        [qkv_total, (small_mine + small_theirs).reshape(-1, 2 * lead)], axis=0
    )
    qkv_total, grad_up_total, grad_out_total = lax.optimization_barrier(
        (qkv_total, grad_up_total, grad_out_total)
    )
    qkv_total = lax.psum(qkv_total, REP)
    qkv_total, small_total = qkv_total[:rows], qkv_total[rows:]
    small_total = small_total.reshape(-1)
    small_out = [small_total[i * rows : (i + 1) * rows] for i in range(8)]
    up_bias_out = small_total[8 * rows : 8 * rows + bias_up.shape[0]]
    return (
        outputs,
        gradient_of_input,
        small_out[0],
        small_out[1],
        qkv_total,
        small_out[6],
        small_out[7],
        grad_out_total,
        small_out[4],
        small_out[2],
        small_out[3],
        grad_up_total,
        up_bias_out,
        total_down_t,
        small_out[5],
    )


def solution(mesh):
    placed = (
        P((SHARD, REP), None),
        P((SHARD, REP)),
        P((SHARD, REP), None),
        P(SHARD),
        P(SHARD),
        P(SHARD, None),
        P(SHARD),
        P(SHARD),
        P(SHARD, None),
        P(SHARD),
        P(SHARD),
        P(SHARD),
        P(SHARD, None),
        P(SHARD),
        P(None, SHARD),
        P(SHARD),
    )

    return jax.shard_map(
        per_device,
        mesh=mesh,
        in_specs=placed,
        out_specs=(
            P((SHARD, REP), None),
            P((SHARD, REP), None),
            P(SHARD),
            P(SHARD),
            P(SHARD, None),
            P(SHARD),
            P(SHARD),
            P(SHARD, None),
            P(SHARD),
            P(SHARD),
            P(SHARD),
            P(SHARD, None),
            P(SHARD),
            P(None, SHARD),
            P(SHARD),
        ),
        check_vma=False,
    )
```
